32 devices in a mesh: tm: 16 (over z, x, core), rows: 2 (over y).
Axes of the slice: x: 2, y: 2, z: 4, core: 2. Of those that a mesh axis runs over, the one named last changes fastest.
Arguments:
- observations: float32 [32, 16, 1024], P('tm', 'rows'), may hold values from -6 to 6
- obs_noise: float32 [32, 16, 1024], P('tm', 'rows'), may hold values from -6 to 6
- prior_noise: float32 [32, 16, 1024], P('tm', 'rows'), may hold values from -4.8 to 4.8
- observed: int32 [32, 16, 1024], P('tm', 'rows'), may hold values 0 or 1
- kappa_sq: float32 [16, 1024], P('rows'), may hold values from 0.5 to 8
- obs_precision: float32 [16, 1024], P('rows'), may hold values from 0.2 to 2
Outputs:
- solution: float32 [32, 16, 1024], P('tm', 'rows')
- residual: float32 [32, 16, 1024], P('tm', 'rows')
- precond: float32 [32, 16, 1024], P('tm', 'rows')
The draws below stay inside these ranges and needn't reach their ends.
All inputs are finite; a program needn't handle non-finite values. No bound on the sum of `observed` on one device may be relied on, other than what follows from the above.
Results may differ from the reference program's by a relative error of at most 0.002.
Values sent between devices are 32-bit elements; how exact they have to be, the bound alone decides.
No kernel may reach another device: no remote copies, remote signals or barrier semaphores. Data moves between devices by JAX's collectives and lax.ppermute only.
A program may use at most 64 MiB of HBM per device.

```python
import math
import jax
import jax.numpy as jnp
from jax import lax

COLS = 1024
ITERS = 2
HOURS = 32
ROWS = 16


def draw_prior_noise(key, part):
    hour_share = jnp.arange(HOURS, dtype=jnp.float32) / float(max(HOURS - 1, 1))
    amplitude = 0.1 + 1.1 * hour_share
    base_values = jnp.clip(jax.random.normal(key, (HOURS, ROWS, COLS), jnp.float32), -4.0, 4.0)
    return (base_values * amplitude[:, None, None]).astype(jnp.float32)


def place_ends(entries, key, low, largest):
    longest = entries.shape.index(max(entries.shape))
    spots = []
    for shift in (0, 1):
        where = [jax.random.randint(jax.random.fold_in(key, axis), (), 0, length) for axis, length in enumerate(entries.shape)]
        where[longest] = (where[longest] + shift) % entries.shape[longest]
        spots.append(tuple(where))
    return entries.at[spots[0]].set(low).at[spots[1]].set(largest)


def steps_of(key, shape, cuts, smallest, top_value):
    def one(position, blocks):
        draws = jax.random.uniform(jax.random.fold_in(jax.random.fold_in(key, 6), position), (blocks,), jnp.float32, smallest / len(cuts), top_value / len(cuts))
        return jnp.repeat(jnp.exp(draws), shape[position] // blocks).reshape((-1,) + (1,) * (len(shape) - position - 1))

    level = one(*cuts[0])
    for cut in cuts[1:]:
        level = level * one(*cut)
    return level


def normal_values(stream_key, shape, spread, bound, cuts=(), kind=jnp.bfloat16):
    array = jax.random.normal(stream_key, shape, jnp.float32) * spread
    if len(cuts) > 0:
        array = steps_of(stream_key, shape, cuts, -0.22, 0.18) * array
    return jnp.clip(array, min=-bound, max=bound).astype(kind)


def setup_inputs(seed: int = 0) -> dict:
    seeds = jax.random.split(jax.random.key(seed), 7)
    return {
        "observations": normal_values(seeds[0], (HOURS, ROWS, COLS), 1.0, 6.0, ((0, 16), (1, 2)), jnp.float32),
        "obs_noise": normal_values(seeds[1], (HOURS, ROWS, COLS), 1.0, 6.0, ((0, 16), (1, 2)), jnp.float32),
        "prior_noise": draw_prior_noise(jax.random.fold_in(seeds[6], 71), 0),
        "observed": place_ends((jax.random.randint(seeds[3], (HOURS, ROWS, COLS), 0, 4) < 1).astype(jnp.int32), jax.random.fold_in(seeds[3], 1), 0, 1),
        "kappa_sq": jnp.clip(jnp.exp(math.log(8.0) - 2.7725887 * jax.random.uniform(seeds[4], (ROWS, COLS), jnp.float32) ** steps_of(seeds[4], (ROWS, COLS), ((0, 2),), -0.2, 0.2)), 0.5, 8.0),
        "obs_precision": jnp.clip(jnp.exp(math.log(2.0) - 2.3025851 * jax.random.uniform(seeds[5], (ROWS, COLS), jnp.float32) ** steps_of(seeds[5], (ROWS, COLS), ((0, 2),), -0.2, 0.2)), 0.2, 2.0),
    }


coupling = 0.995

def hour_weights(count):
    inner = jnp.full((count,), 1.0 + coupling * coupling, jnp.float32)
    return inner.at[0].set(1.0).at[count - 1].set(1.0)

def operate(field, stencil_diag, weights, obs_weight):
    padded = jnp.pad(field, ((0, 0), (1, 1), (1, 1)))
    beside = padded[:, 2:, 1:-1] + padded[:, :-2, 1:-1] + padded[:, 1:-1, 2:] + padded[:, 1:-1, :-2]
    spatial = stencil_diag * field - beside
    hour_pad = jnp.pad(spatial, ((1, 1), (0, 0), (0, 0)))
    return weights * spatial - coupling * (hour_pad[2:] + hour_pad[:-2]) + obs_weight * field

def solve_hours(right_hand_part, main_diagonal_entries, offdiagonal_entries):

    def downward_solve(current_state, matrix_entries):
        previous_ratio, previous_elimination = current_state
        forcing_row, main_row = matrix_entries
        pivot_entry = main_row - offdiagonal_entries * previous_ratio
        current_ratio = offdiagonal_entries / pivot_entry
        current_elimination = (forcing_row - offdiagonal_entries * previous_elimination) / pivot_entry
        return ((current_ratio, current_elimination), (current_ratio, current_elimination))
    empty_field_grid = jnp.zeros_like(offdiagonal_entries)
    unused_item, (multiplier_list, elimination_list) = lax.scan(downward_solve, (empty_field_grid, empty_field_grid), (right_hand_part, main_diagonal_entries))

    def upward_solve(following_value, matrix_entries):
        multiplier_row, elimination_row = matrix_entries
        current_value = elimination_row - multiplier_row * following_value
        return (current_value, current_value)
    unused_item, value_list = lax.scan(upward_solve, empty_field_grid, (multiplier_list, elimination_list), reverse=True)
    return value_list

def reference(observations, obs_noise, prior_noise, observed, kappa_sq, obs_precision):
    maskf = observed.astype(jnp.float32)
    obs_weight = maskf * obs_precision
    right = maskf * (obs_precision * observations + jnp.sqrt(obs_precision) * obs_noise) + prior_noise
    stencil_diag = kappa_sq + 4.0
    weights = hour_weights(HOURS)[:, None, None]
    main_diagonal_entries = weights * stencil_diag + obs_weight
    offdiagonal_entries = -coupling * stencil_diag
    solution = jnp.zeros_like(right)
    residual = right
    precond = solve_hours(residual, main_diagonal_entries, offdiagonal_entries)
    direction = precond
    aligned = jnp.sum(residual * precond)
    for iteration in range(ITERS):
        applied = operate(direction, stencil_diag, weights, obs_weight)
        step_size = aligned / jnp.sum(direction * applied)
        solution = solution + step_size * direction
        residual = residual - step_size * applied
        precond = solve_hours(residual, main_diagonal_entries, offdiagonal_entries)
        aligned_new = jnp.sum(residual * precond)
        direction = precond + aligned_new / aligned * direction
        aligned = aligned_new
    return (solution, residual, precond)
```

```python
import jax
import jax.numpy as jnp
from jax import lax
from jax.sharding import PartitionSpec as P

ITERS = 2
coupling = 0.995
AXES = ("tm", "rows")


def column_windows(field, blocks, halo):
    width = field.shape[-1] // blocks
    split = field.shape[:-1] + (blocks, width)
    parts = []
    for step in range(halo, 0, -1):
        moved = jnp.pad(field, [(0, 0)] * (field.ndim - 1) + [(step, 0)])[..., : field.shape[-1]]
        parts.append(moved.reshape(split)[..., :1])
    parts.append(field.reshape(split))
    for step in range(1, halo + 1):
        moved = jnp.pad(field, [(0, 0)] * (field.ndim - 1) + [(0, step)])[..., step:]
        parts.append(moved.reshape(split)[..., -1:])
    return jnp.concatenate(parts, axis=-1)


def hour_factors(main, off):
    def advance(inverse, row):
        inverse = 1.0 / (row - off * off * inverse)
        return inverse, inverse

    return lax.scan(advance, jnp.zeros_like(off), main)[1]


def hour_solve(right, inverse, ratio):
    def down(before, entries):
        value, inv, rat = entries
        now = value * inv - rat * before
        return now, now

    def up(after, entries):
        value, rat = entries
        now = value - rat * after
        return now, now

    zero = jnp.zeros_like(right[0])
    forward = lax.scan(down, zero, (right, inverse, ratio))[1]
    return lax.scan(up, zero, (forward, ratio), reverse=True)[1]


def split_off(field, weights):
    padded = jnp.pad(field, ((0, 0), (1, 1), (1, 1)))
    beside = padded[:, 2:, 1:-1] + padded[:, :-2, 1:-1] + padded[:, 1:-1, 2:] + padded[:, 1:-1, :-2]
    hours = jnp.pad(beside, ((1, 1), (0, 0), (0, 0)))
    return weights * beside - coupling * (hours[2:] + hours[:-2])


def step_scalars(a, h, hp, k, m, n):
    alpha = a / (a - h)
    delta = -h / (a - h)
    rz = delta * delta * a + alpha * delta * (h + hp) + alpha * alpha * k
    g = delta + rz / a
    curve = g * g * (a - h) + g * alpha * (h - m + hp - k) + alpha * alpha * (k - n)
    beta = rz / curve
    return alpha + beta * g, beta * alpha, delta - beta * g, alpha + beta * g - beta * alpha


def per_device(observations, obs_noise, prior_noise, observed, kappa_sq, obs_precision):
    hours, rows, columns = observations.shape
    over_tm, over_rows = lax.axis_size("tm"), lax.axis_size("rows")
    blocks = over_tm * over_rows
    width = columns // blocks
    wide = width + 2 * ITERS
    mask = observed.astype(jnp.float32)
    obs_weight = mask * obs_precision
    right = (
        mask * (obs_precision * observations + jnp.sqrt(obs_precision) * obs_noise) + prior_noise
    )
    payload = jnp.concatenate([right, obs_weight, kappa_sq[None]], axis=0)
    payload = jnp.moveaxis(column_windows(payload, blocks, ITERS), 2, 0)
    payload = payload.reshape(blocks, -1)
    got = lax.all_to_all(payload, AXES, split_axis=0, concat_axis=0, tiled=True)
    got = got.reshape(over_tm, over_rows, 2 * hours + 1, rows, wide)
    got = jnp.moveaxis(got, 2, 1)
    all_rows = over_rows * rows
    every = over_tm * hours
    r0 = got[:, :hours].reshape(every, all_rows, wide)
    ow = got[:, hours : 2 * hours].reshape(every, all_rows, wide)
    diag = got[0, 2 * hours].reshape(all_rows, wide) + 4.0
    where = (lax.axis_index("tm") * over_rows + lax.axis_index("rows")) * width
    column = where - ITERS + jnp.arange(wide, dtype=jnp.int32)
    inside = (column >= 0) & (column < columns)
    hour = jnp.arange(every)
    ends = (hour == 0) | (hour == every - 1)
    weights = jnp.where(ends, 1.0, 1.0 + coupling * coupling).astype(jnp.float32)[:, None, None]
    off = -coupling * diag
    inverse = hour_factors(weights * diag + ow, off)
    ratio = off * inverse
    z0 = hour_solve(r0, inverse, ratio)
    s1 = jnp.where(inside, split_off(z0, weights), 0.0)
    y1 = hour_solve(s1, inverse, ratio)
    s2 = jnp.where(inside, split_off(y1, weights), 0.0)
    y2 = hour_solve(s2, inverse, ratio)
    own = slice(ITERS, ITERS + width)
    r0, z0, s1, y1, s2, y2 = (part[:, :, own] for part in (r0, z0, s1, y1, s2, y2))
    pairs = ((r0, z0), (z0, s1), (r0, y1), (s1, y1), (z0, s2), (y1, s2))
    sums = jnp.stack([jnp.sum(x * y) for x, y in pairs])
    back = jnp.stack([z0, y1, y2, s1, s2]).reshape(-1, over_tm, hours, over_rows, rows, width)
    items = back.shape[0]
    back = back.transpose(1, 3, 0, 2, 4, 5).reshape(blocks, -1)
    back = jnp.concatenate([back, jnp.broadcast_to(sums, (blocks, sums.shape[0]))], axis=1)
    got = lax.all_to_all(back, AXES, split_axis=0, concat_axis=0, tiled=True)
    sums = jnp.sum(got[:, -sums.shape[0] :], axis=0)
    got = got[:, : -sums.shape[0]].reshape(blocks, items, hours, rows, width)
    z0, y1, y2, s1, s2 = got.transpose(1, 2, 3, 0, 4).reshape(items, hours, rows, columns)
    cx, c2, c0, c1 = step_scalars(*sums)
    return (
        cx * z0 + c2 * y1,
        c0 * right + c1 * s1 + c2 * s2,
        c0 * z0 + c1 * y1 + c2 * y2,
    )


def solution(mesh):
    whole, plane = P("tm", "rows", None), P("rows", None)
    return jax.shard_map(
        per_device,
        mesh=mesh,
        in_specs=(whole, whole, whole, whole, plane, plane),
        out_specs=(whole, whole, whole),
        check_vma=False,
    )
```

```python
import jax
import jax.numpy as jnp
from jax import lax
from jax.experimental import pallas as pl
from jax.experimental.pallas import tpu as pltpu
from jax.sharding import PartitionSpec as P

ITERS = 2
coupling = 0.995
AXES = ("tm", "rows")


def column_windows(field, blocks, halo):
    width = field.shape[-1] // blocks
    split = field.shape[:-1] + (blocks, width)
    parts = []
    for step in range(halo, 0, -1):
        moved = jnp.pad(field, [(0, 0)] * (field.ndim - 1) + [(step, 0)])[..., : field.shape[-1]]
        parts.append(moved.reshape(split)[..., :1])
    parts.append(field.reshape(split))
    for step in range(1, halo + 1):
        moved = jnp.pad(field, [(0, 0)] * (field.ndim - 1) + [(0, step)])[..., step:]
        parts.append(moved.reshape(split)[..., -1:])
    return jnp.concatenate(parts, axis=-1)


def hour_factors(main, off):
    def advance(inverse, row):
        inverse = 1.0 / (row - off * off * inverse)
        return inverse, inverse

    return lax.scan(advance, jnp.zeros_like(off), main)[1]


def hour_solve(right, inverse, ratio):
    def down(before, entries):
        value, inv, rat = entries
        now = value * inv - rat * before
        return now, now

    def up(after, entries):
        value, rat = entries
        now = value - rat * after
        return now, now

    zero = jnp.zeros_like(right[0])
    forward = lax.scan(down, zero, (right, inverse, ratio))[1]
    return lax.scan(up, zero, (forward, ratio), reverse=True)[1]


def split_off(field, weights):
    padded = jnp.pad(field, ((0, 0), (1, 1), (1, 1)))
    beside = padded[:, 2:, 1:-1] + padded[:, :-2, 1:-1] + padded[:, 1:-1, 2:] + padded[:, 1:-1, :-2]
    hours = jnp.pad(beside, ((1, 1), (0, 0), (0, 0)))
    return weights * beside - coupling * (hours[2:] + hours[:-2])


def step_scalars(a, h, hp, k, m, n):
    alpha = a / (a - h)
    delta = -h / (a - h)
    rz = delta * delta * a + alpha * delta * (h + hp) + alpha * alpha * k
    g = delta + rz / a
    curve = g * g * (a - h) + g * alpha * (h - m + hp - k) + alpha * alpha * (k - n)
    beta = rz / curve
    return alpha + beta * g, beta * alpha, delta - beta * g, alpha + beta * g - beta * alpha


def per_device_any(observations, obs_noise, prior_noise, observed, kappa_sq, obs_precision):
    hours, rows, columns = observations.shape
    over_tm, over_rows = lax.axis_size("tm"), lax.axis_size("rows")
    blocks = over_tm * over_rows
    width = columns // blocks
    wide = width + 2 * ITERS
    mask = observed.astype(jnp.float32)
    obs_weight = mask * obs_precision
    right = (
        mask * (obs_precision * observations + jnp.sqrt(obs_precision) * obs_noise) + prior_noise
    )
    payload = jnp.concatenate([right, obs_weight, kappa_sq[None]], axis=0)
    payload = jnp.moveaxis(column_windows(payload, blocks, ITERS), 2, 0)
    payload = payload.reshape(blocks, -1)
    got = lax.all_to_all(payload, AXES, split_axis=0, concat_axis=0, tiled=True)
    got = got.reshape(over_tm, over_rows, 2 * hours + 1, rows, wide)
    got = jnp.moveaxis(got, 2, 1)
    all_rows = over_rows * rows
    every = over_tm * hours
    r0 = got[:, :hours].reshape(every, all_rows, wide)
    ow = got[:, hours : 2 * hours].reshape(every, all_rows, wide)
    diag = got[0, 2 * hours].reshape(all_rows, wide) + 4.0
    where = (lax.axis_index("tm") * over_rows + lax.axis_index("rows")) * width
    column = where - ITERS + jnp.arange(wide, dtype=jnp.int32)
    inside = (column >= 0) & (column < columns)
    hour = jnp.arange(every)
    ends = (hour == 0) | (hour == every - 1)
    weights = jnp.where(ends, 1.0, 1.0 + coupling * coupling).astype(jnp.float32)[:, None, None]
    off = -coupling * diag
    inverse = hour_factors(weights * diag + ow, off)
    ratio = off * inverse
    z0 = hour_solve(r0, inverse, ratio)
    s1 = jnp.where(inside, split_off(z0, weights), 0.0)
    y1 = hour_solve(s1, inverse, ratio)
    s2 = jnp.where(inside, split_off(y1, weights), 0.0)
    y2 = hour_solve(s2, inverse, ratio)
    own = slice(ITERS, ITERS + width)
    r0, z0, s1, y1, s2, y2 = (part[:, :, own] for part in (r0, z0, s1, y1, s2, y2))
    pairs = ((r0, z0), (z0, s1), (r0, y1), (s1, y1), (z0, s2), (y1, s2))
    sums = jnp.stack([jnp.sum(x * y) for x, y in pairs])
    back = jnp.stack([z0, y1, y2, s1, s2]).reshape(-1, over_tm, hours, over_rows, rows, width)
    items = back.shape[0]
    back = back.transpose(1, 3, 0, 2, 4, 5).reshape(blocks, -1)
    back = jnp.concatenate([back, jnp.broadcast_to(sums, (blocks, sums.shape[0]))], axis=1)
    got = lax.all_to_all(back, AXES, split_axis=0, concat_axis=0, tiled=True)
    sums = jnp.sum(got[:, -sums.shape[0] :], axis=0)
    got = got[:, : -sums.shape[0]].reshape(blocks, items, hours, rows, width)
    z0, y1, y2, s1, s2 = got.transpose(1, 2, 3, 0, 4).reshape(items, hours, rows, columns)
    cx, c2, c0, c1 = step_scalars(*sums)
    return (
        cx * z0 + c2 * y1,
        c0 * right + c1 * s1 + c2 * s2,
        c0 * z0 + c1 * y1 + c2 * y2,
    )


LANES, SUB = 128, 8
HALF = LANES // 2
PAD = 4


def lanes_of():
    lane = lax.broadcasted_iota(jnp.int32, (SUB, LANES), 1)
    sub = lax.broadcasted_iota(jnp.int32, (SUB, LANES), 0)
    return lane, sub


def turn(x, shift):
    shift = shift % LANES
    return x if shift == 0 else pltpu.roll(x, shift, 1)


def pack_kernel(blocks, obs, noise, prior, observed, kappa, precision, right, out, weight):
    hours, _, columns = obs.shape
    width = columns // blocks
    lane, _ = lanes_of()
    prec = precision[...]
    root = jnp.sqrt(prec)
    for h in range(hours):
        mask = observed[h].astype(jnp.float32)
        right[h] = mask * (prec * obs[h] + root * noise[h]) + prior[h]
        weight[h] = mask * prec
    zero = jnp.zeros((SUB, LANES), jnp.float32)

    def tile(ref, k):
        inside = 0 <= k < columns // LANES
        return ref[:, k * LANES : (k + 1) * LANES] if inside else zero

    def window(ref, block):
        k, at = divmod(block * width, LANES)
        here = tile(ref, k)
        if at < ITERS:
            here = jnp.where(lane >= HALF, tile(ref, k - 1), here)
        if at + width + ITERS > LANES:
            here = jnp.where(lane < HALF, tile(ref, k + 1), here)
        return here, at

    low = lax.rem(lane + PAD, LANES) < HALF
    spot = width + ITERS + PAD
    piece = width // 2 + ITERS
    third = (lane >= spot - 1) & (lane < HALF - PAD)
    for block in range(blocks):
        kap, at = window(kappa, block)
        for h in range(hours):
            lo = turn(window(right.at[h], block)[0], -at)
            hi = turn(window(weight.at[h], block)[0], HALF - at)
            chunk = jnp.where(low, lo, hi)
            if h < 2:
                chunk = jnp.where(third, turn(kap, spot - (at - ITERS + h * piece)), chunk)
            out[block, h] = chunk


def solve_kernel(columns, got, out, right, inv, rat, z0, y1, y2, s1, s2):
    blocks, hb = got.shape[:2]
    strips = 2
    every = blocks // strips * hb
    width = columns // blocks
    half = every // 2
    lane, sub = lanes_of()
    low = lax.rem(lane + PAD, LANES) < HALF
    place = lax.rem(lane + PAD, HALF) - PAD
    block = lax.axis_index("tm") * strips + lax.axis_index("rows")
    column = block * width + place
    inside = (place >= -ITERS) & (place < width + ITERS) & (column >= 0) & (column < columns)
    own = (place >= 0) & (place < width)
    spot = width + ITERS + PAD
    piece = width // 2 + ITERS

    def pieces(h):
        return jnp.where(low, got[0, h], turn(got[1, h], HALF))

    kap = jnp.where(
        place < piece - ITERS, turn(pieces(0), -ITERS - spot), turn(pieces(1), piece - ITERS - spot)
    )
    window = (place >= -ITERS) & (place < width + ITERS)
    diag = jnp.where(window, kap, 0.0) + 4.0
    off = -coupling * diag
    off_sq = off * off
    inner = (1.0 + coupling * coupling) * diag
    zero = jnp.zeros((SUB, LANES), jnp.float32)

    def hour_weight(t):
        return 1.0 if t in (0, every - 1) else 1.0 + coupling * coupling

    order = [(i, every - 1 - i) for i in range(half)]
    before = [None, None]
    for both in order:
        for side, t in enumerate(both):
            src, h = divmod(t, hb)
            c0, c1 = got[strips * src, h], got[strips * src + 1, h]
            rhs = jnp.where(low, c0, turn(c1, HALF))
            main = jnp.where(low, turn(c0, HALF), c1) + (
                diag if t in (0, every - 1) else inner
            )
            pivot = main if before[side] is None else main - off_sq * before[side][0]
            iv = 1.0 / pivot
            c = off * iv
            g = rhs * iv if before[side] is None else rhs * iv - c * before[side][1]
            right[t], inv[t], rat[t], z0[t] = rhs, iv, c, g
            before[side] = (iv, g)
    top, low_t = half - 1, half
    joint = 1.0 / (1.0 - rat[top] * rat[low_t])

    def outward(ref):
        c_top, c_low = rat[top], rat[low_t]
        a = (ref[top] - c_top * ref[low_t]) * joint
        b = ref[low_t] - c_low * a
        ref[top], ref[low_t] = a, b
        for i in range(1, half):
            a = ref[top - i] - rat[top - i] * a
            b = ref[low_t + i] - rat[low_t + i] * b
            ref[top - i], ref[low_t + i] = a, b

    def inward(source, ref):
        a = b = None
        for i, j in order:
            a = source[i] * inv[i] if a is None else source[i] * inv[i] - rat[i] * a
            b = source[j] * inv[j] if b is None else source[j] * inv[j] - rat[j] * b
            ref[i], ref[j] = a, b

    last, initial = sub == SUB - 1, sub == 0
    edge = (last & ~low) | (initial & low)

    def beside(v):
        across = jnp.where(edge, turn(v, HALF), 0.0)
        up = pltpu.roll(jnp.where(last, across, v), 1, 0)
        down = pltpu.roll(jnp.where(initial, across, v), SUB - 1, 0)
        return (up + down) + (turn(v, 1) + turn(v, -1))

    def split(ref, result):
        old, now = zero, beside(ref[0])
        for t in range(every):
            new = beside(ref[t + 1]) if t + 1 < every else zero
            value = hour_weight(t) * now - coupling * (old + new)
            result[t] = jnp.where(inside, value, 0.0)
            old, now = now, new

    outward(z0)
    split(z0, s1)
    inward(s1, y1)
    outward(y1)
    split(y1, s2)
    inward(s2, y2)
    outward(y2)

    total = zero
    pairs = ((right, z0), (z0, s1), (right, y1), (s1, y1), (z0, s2), (y1, s2))
    for row, (x, y) in enumerate(pairs):
        parts = [x[t] * y[t] for t in range(4)]
        for t in range(4, every):
            parts[t % 4] = parts[t % 4] + x[t] * y[t]
        part = jnp.where(own, (parts[0] + parts[1]) + (parts[2] + parts[3]), 0.0)
        part = jnp.sum(part, axis=0, keepdims=True)
        total = jnp.where(sub == row, part, total)
    total = total + turn(total, HALF)

    first = lax.rem(lane, HALF) < HALF // 2
    left = lane < HALF

    def two(a, b):
        return jnp.where(first, a, turn(b, HALF // 2))

    total = two(total, zero)
    for src in range(blocks // strips):
        t = src * hb
        groups = (
            (two(z0[t], z0[t + 1]), two(s1[t], s1[t + 1])),
            (two(y1[t], y1[t + 1]), two(s2[t], s2[t + 1])),
            (two(y2[t], y2[t + 1]), total),
        )
        for g, (a, b) in enumerate(groups):
            out[strips * src, g] = jnp.where(left, a, turn(b, HALF))
            out[strips * src + 1, g] = jnp.where(left, turn(a, HALF), b)


def unpack_kernel(got, right, solution, residual, precond):
    blocks = got.shape[0]
    lane, _ = lanes_of()
    left = lane < HALF
    first = lax.rem(lane, HALF) < HALF // 2
    parts = [got[c, 2] for c in range(4)]
    for c in range(4, blocks):
        parts[c % 4] = parts[c % 4] + got[c, 2]
    total = (parts[0] + parts[1]) + (parts[2] + parts[3])
    total = jnp.sum(jnp.where(left, 0.0, total), axis=1, keepdims=True)
    total = jnp.broadcast_to(total, (SUB, LANES))
    sums = [jnp.broadcast_to(total[i : i + 1], (SUB, LANES)) for i in range(6)]
    cx, c2, c0, c1 = step_scalars(*sums)
    k0, k1, k2 = jnp.where(left, c0, c1), jnp.where(left, c1, c2), jnp.where(left, c2, 0.0)
    per = 4
    for tile in range(blocks // per):
        at = pl.ds(tile * LANES, LANES)
        mixed, iterate = [], []
        for c in range(tile * per, tile * per + per):
            v0, v1, v2 = got[c, 0], got[c, 1], got[c, 2]
            mixed.append(k0 * v0 + k1 * v1 + k2 * v2)
            iterate.append(cx * v0 + c2 * v1)

        def heads(q):
            return [jnp.where(left, q[i], turn(q[i + 2], HALF)) for i in (0, 1)]

        def tails(q):
            return [jnp.where(left, turn(q[i], HALF), q[i + 2]) for i in (0, 1)]

        def spread(p):
            step = HALF // 2
            return (
                jnp.where(first, p[0], turn(p[1], step)),
                jnp.where(first, turn(p[0], -step), p[1]),
            )

        for h, value in enumerate(spread(heads(iterate))):
            solution[h, :, at] = value
        for h, value in enumerate(spread(heads(mixed))):
            precond[h, :, at] = value
        for h, value in enumerate(spread(tails(mixed))):
            residual[h, :, at] = c0 * right[h, :, at] + value


def per_device(observations, obs_noise, prior_noise, observed, kappa_sq, obs_precision):
    hours, rows, columns = observations.shape
    blocks = lax.axis_size("tm") * lax.axis_size("rows")
    fits = (
        lax.axis_size("rows") == 2
        and hours == 2
        and rows == SUB
        and columns % LANES == 0
        and columns == blocks * (LANES // 4)
    )
    args = (observations, obs_noise, prior_noise, observed, kappa_sq, obs_precision)
    if not fits:
        return per_device_any(*args)
    every = blocks // 2 * hours

    def shaped(*shape):
        return jax.ShapeDtypeStruct(shape, jnp.float32)

    right, chunks = pl.pallas_call(
        lambda *refs: pack_kernel(blocks, *refs),
        out_shape=(shaped(hours, rows, columns), shaped(blocks, hours, rows, LANES)),
        scratch_shapes=[pltpu.VMEM((hours, rows, columns), jnp.float32)],
        name="pack",
    )(*args)
    got = lax.all_to_all(chunks, AXES, split_axis=0, concat_axis=0, tiled=True)
    chunks = pl.pallas_call(
        lambda *refs: solve_kernel(columns, *refs),
        out_shape=shaped(blocks, 3, rows, LANES),
        scratch_shapes=[pltpu.VMEM((every, rows, LANES), jnp.float32)] * 8,
        name="solve",
    )(got)
    got = lax.all_to_all(chunks, AXES, split_axis=0, concat_axis=0, tiled=True)
    return tuple(
        pl.pallas_call(
            unpack_kernel,
            out_shape=[shaped(hours, rows, columns)] * 3,
            name="unpack",
        )(got, right)
    )


def solution(mesh):
    whole, plane = P("tm", "rows", None), P("rows", None)
    return jax.shard_map(
        per_device,
        mesh=mesh,
        in_specs=(whole, whole, whole, whole, plane, plane),
        out_specs=(whole, whole, whole),
        check_vma=False,
    )
```

```python
import jax
import jax.numpy as jnp
from jax import lax
from jax.experimental import pallas as pl
from jax.experimental.pallas import tpu as pltpu
from jax.sharding import PartitionSpec as P

ITERS = 2
coupling = 0.995
AXES = ("tm", "rows")


def column_windows(field, blocks, halo):
    width = field.shape[-1] // blocks
    split = field.shape[:-1] + (blocks, width)
    parts = []
    for step in range(halo, 0, -1):
        moved = jnp.pad(field, [(0, 0)] * (field.ndim - 1) + [(step, 0)])[..., : field.shape[-1]]
        parts.append(moved.reshape(split)[..., :1])
    parts.append(field.reshape(split))
    for step in range(1, halo + 1):
        moved = jnp.pad(field, [(0, 0)] * (field.ndim - 1) + [(0, step)])[..., step:]
        parts.append(moved.reshape(split)[..., -1:])
    return jnp.concatenate(parts, axis=-1)


def hour_factors(main, off):
    def advance(inverse, row):
        inverse = 1.0 / (row - off * off * inverse)
        return inverse, inverse

    return lax.scan(advance, jnp.zeros_like(off), main)[1]


def hour_solve(right, inverse, ratio):
    def down(before, entries):
        value, inv, rat = entries
        now = value * inv - rat * before
        return now, now

    def up(after, entries):
        value, rat = entries
        now = value - rat * after
        return now, now

    zero = jnp.zeros_like(right[0])
    forward = lax.scan(down, zero, (right, inverse, ratio))[1]
    return lax.scan(up, zero, (forward, ratio), reverse=True)[1]


def split_off(field, weights):
    padded = jnp.pad(field, ((0, 0), (1, 1), (1, 1)))
    beside = padded[:, 2:, 1:-1] + padded[:, :-2, 1:-1] + padded[:, 1:-1, 2:] + padded[:, 1:-1, :-2]
    hours = jnp.pad(beside, ((1, 1), (0, 0), (0, 0)))
    return weights * beside - coupling * (hours[2:] + hours[:-2])


def step_scalars(a, h, hp, k, m, n):
    alpha = a / (a - h)
    delta = -h / (a - h)
    rz = delta * delta * a + alpha * delta * (h + hp) + alpha * alpha * k
    g = delta + rz / a
    curve = g * g * (a - h) + g * alpha * (h - m + hp - k) + alpha * alpha * (k - n)
    beta = rz / curve
    return alpha + beta * g, beta * alpha, delta - beta * g, alpha + beta * g - beta * alpha


def per_device_any(observations, obs_noise, prior_noise, observed, kappa_sq, obs_precision):
    hours, rows, columns = observations.shape
    over_tm, over_rows = lax.axis_size("tm"), lax.axis_size("rows")
    blocks = over_tm * over_rows
    width = columns // blocks
    wide = width + 2 * ITERS
    mask = observed.astype(jnp.float32)
    obs_weight = mask * obs_precision
    right = (
        mask * (obs_precision * observations + jnp.sqrt(obs_precision) * obs_noise) + prior_noise
    )
    payload = jnp.concatenate([right, obs_weight, kappa_sq[None]], axis=0)
    payload = jnp.moveaxis(column_windows(payload, blocks, ITERS), 2, 0)
    payload = payload.reshape(blocks, -1)
    got = lax.all_to_all(payload, AXES, split_axis=0, concat_axis=0, tiled=True)
    got = got.reshape(over_tm, over_rows, 2 * hours + 1, rows, wide)
    got = jnp.moveaxis(got, 2, 1)
    all_rows = over_rows * rows
    every = over_tm * hours
    r0 = got[:, :hours].reshape(every, all_rows, wide)
    ow = got[:, hours : 2 * hours].reshape(every, all_rows, wide)
    diag = got[0, 2 * hours].reshape(all_rows, wide) + 4.0
    where = (lax.axis_index("tm") * over_rows + lax.axis_index("rows")) * width
    column = where - ITERS + jnp.arange(wide, dtype=jnp.int32)
    inside = (column >= 0) & (column < columns)
    hour = jnp.arange(every)
    ends = (hour == 0) | (hour == every - 1)
    weights = jnp.where(ends, 1.0, 1.0 + coupling * coupling).astype(jnp.float32)[:, None, None]
    off = -coupling * diag
    inverse = hour_factors(weights * diag + ow, off)
    ratio = off * inverse
    z0 = hour_solve(r0, inverse, ratio)
    s1 = jnp.where(inside, split_off(z0, weights), 0.0)
    y1 = hour_solve(s1, inverse, ratio)
    s2 = jnp.where(inside, split_off(y1, weights), 0.0)
    y2 = hour_solve(s2, inverse, ratio)
    own = slice(ITERS, ITERS + width)
    r0, z0, s1, y1, s2, y2 = (part[:, :, own] for part in (r0, z0, s1, y1, s2, y2))
    pairs = ((r0, z0), (z0, s1), (r0, y1), (s1, y1), (z0, s2), (y1, s2))
    sums = jnp.stack([jnp.sum(x * y) for x, y in pairs])
    back = jnp.stack([z0, y1, y2, s1, s2]).reshape(-1, over_tm, hours, over_rows, rows, width)
    items = back.shape[0]
    back = back.transpose(1, 3, 0, 2, 4, 5).reshape(blocks, -1)
    back = jnp.concatenate([back, jnp.broadcast_to(sums, (blocks, sums.shape[0]))], axis=1)
    got = lax.all_to_all(back, AXES, split_axis=0, concat_axis=0, tiled=True)
    sums = jnp.sum(got[:, -sums.shape[0] :], axis=0)
    got = got[:, : -sums.shape[0]].reshape(blocks, items, hours, rows, width)
    z0, y1, y2, s1, s2 = got.transpose(1, 2, 3, 0, 4).reshape(items, hours, rows, columns)
    cx, c2, c0, c1 = step_scalars(*sums)
    return (
        cx * z0 + c2 * y1,
        c0 * right + c1 * s1 + c2 * s2,
        c0 * z0 + c1 * y1 + c2 * y2,
    )


LANES, SUB = 128, 8
HALF = LANES // 2
SLOTS = 4
SLOT = LANES // SLOTS
EXTRA = 2


def lanes_of():
    lane = lax.broadcasted_iota(jnp.int32, (SUB, LANES), 1)
    sub = lax.broadcasted_iota(jnp.int32, (SUB, LANES), 0)
    return lane, sub


def turn(x, shift):
    shift = shift % LANES
    return x if shift == 0 else pltpu.roll(x, shift, 1)


def halves(a, b, left):
    return jnp.where(left, a, turn(b, HALF)), jnp.where(left, turn(a, HALF), b)


def quad(q, left, first):
    p0, p2 = halves(q[0], q[2], left)
    p1, p3 = halves(q[1], q[3], left)
    result = []
    for a, b in ((p0, p1), (p2, p3)):
        result.append(jnp.where(first, a, turn(b, SLOT)))
        result.append(jnp.where(first, turn(a, -SLOT), b))
    return result


def tile(ref, k, *row):
    at = pl.ds(k * LANES, LANES)
    return ref[row + (slice(None), at)] if row else ref[:, at]


def pack_kernel(obs, noise, prior, observed, kappa, precision, right, weight, out):
    hours, _, columns = obs.shape
    tiles = columns // LANES
    blocks = tiles * SLOTS
    lane, sub = lanes_of()
    left = lane < HALF
    slot_lane = lax.rem(lane, SLOT)
    first = lax.rem(lane, HALF) < SLOT
    rows = SUB + EXTRA
    prec = precision[...]
    root = jnp.sqrt(prec)
    for h in range(hours):
        mask = observed[h].astype(jnp.float32)
        right[h] = mask * (prec * obs[h] + root * noise[h]) + prior[h]
        weight[h] = mask * prec
    zero = jnp.zeros((SUB, LANES), jnp.float32)

    span = 2 * ITERS
    beginnings, endings = [], []
    for k in range(tiles):
        items = [tile(ref, k, h) for ref in (right, weight) for h in range(hours)]
        for j, chunk in enumerate(quad(items, left, first)):
            out[pl.ds((k * SLOTS + j) * rows, SUB), :] = chunk
        begin, end = zero, zero
        for i, item in enumerate(items):
            at = i * span
            begin = jnp.where(slot_lane // ITERS == i * 2 + 1, turn(item, at + ITERS), begin)
            end = jnp.where(slot_lane // ITERS == i * 2, turn(item, at - SLOT + ITERS), end)
        falling = lax.rem(SUB - sub, SUB)
        beginnings.append(jnp.take_along_axis(begin, falling, axis=0))
        endings.append(jnp.take_along_axis(end, falling, axis=0))

    line = lax.rem(lax.axis_index("tm"), SUB)
    kap = [
        jnp.sum(jnp.where(sub == line, tile(kappa, k), 0.0), axis=0, keepdims=True)
        for k in range(tiles)
    ]
    wide = len(items) * span
    before = lax.rem(lane // ITERS, 2) == 0
    lane_row = lax.broadcasted_iota(jnp.int32, (1, LANES), 1)
    for block in range(blocks):
        k, j = divmod(block, SLOTS)
        at = j * SLOT
        prev = turn(endings[(block - 1) // SLOTS], SLOT - at) if block else zero
        last = block == blocks - 1
        follow = zero if last else turn(beginnings[(block + 1) // SLOTS], -at - SLOT)
        halo = jnp.where(lane < wide, jnp.where(before, prev, follow), 0.0)
        halo = pltpu.roll(halo, 0, 1, stride=wide, stride_axis=0)
        out[pl.ds(block * rows + SUB, 1), :] = jnp.sum(halo, axis=0, keepdims=True)
        here = kap[k]
        if j == 0 and k > 0:
            here = jnp.where(lane_row >= HALF, kap[k - 1], here)
        if j == SLOTS - 1 and k + 1 < tiles:
            here = jnp.where(lane_row < HALF, kap[k + 1], here)
        out[pl.ds(block * rows + SUB + 1, 1), :] = turn(here, -at)


def solve_kernel(columns, got, out, right, inv, rat, z0, y1, y2, s1, s2, side):
    strips, hb = 2, 2
    rows = SUB + EXTRA
    blocks = got.shape[0] // rows
    pairs = blocks // strips
    every = pairs * hb
    width = SLOT
    half = every // 2
    lane, sub = lanes_of()
    left = lane < HALF
    first = lax.rem(lane, HALF) < SLOT
    low = lax.rem(lane + ITERS, LANES) < HALF
    place = lax.rem(lane + ITERS, HALF) - ITERS
    block = lax.axis_index("tm") * strips + lax.axis_index("rows")
    column = block * width + place
    window = place < width + ITERS
    inside = window & (column >= 0) & (column < columns)
    own = (place >= 0) & (place < width)
    ahead = place < 0
    zero = jnp.zeros((SUB, LANES), jnp.float32)

    def strip_rows(at):
        return [jnp.broadcast_to(got[pl.ds(at + s * rows, 1), :], (SUB, LANES)) for s in (0, 1)]

    kap = [zero, zero]
    for i in range(SUB):
        lines = strip_rows(i * strips * rows + SUB + 1)
        kap = [jnp.where(sub == i, line, k) for line, k in zip(lines, kap)]
    kap = jnp.where(low, kap[0], turn(kap[1], HALF))
    diag = jnp.where(window, kap, 0.0) + 4.0
    off = -coupling * diag
    off_sq = off * off
    inner = (1.0 + coupling * coupling) * diag

    span = 2 * ITERS
    wide = 2 * hb * span

    def fields(pair):
        at = pair * strips * rows
        c0, c1 = got[pl.ds(at, SUB), :], got[pl.ds(at + rows, SUB), :]
        h0, h1 = (
            pltpu.roll(line, 0, 1, stride=wide, stride_axis=0)
            for line in strip_rows(at + SUB)
        )
        halo = jnp.where(left, h0, turn(h1, HALF))
        result = []
        for i, mine in enumerate(halves(c0, c1, left)):
            for h in range(hb):
                item = i * hb + h
                around = jnp.where(
                    ahead,
                    turn(halo, -ITERS - item * span),
                    turn(halo, SLOT - ITERS - item * span),
                )
                result.append(jnp.where(own, turn(mine, -h * SLOT), around))
        return result

    def hour_weight(t):
        return 1.0 if t in (0, every - 1) else 1.0 + coupling * coupling

    def eliminate(t, rhs, weight, before):
        main = jnp.where(window, weight, 0.0) + (diag if t in (0, every - 1) else inner)
        pivot = main if before is None else main - off_sq * before[0]
        iv = 1.0 / pivot
        c = off * iv
        g = rhs * iv if before is None else rhs * iv - c * before[1]
        right[t], inv[t], rat[t], z0[t] = rhs, iv, c, g
        return iv, g

    upper = lower = None
    for i in range(0, half, hb):
        r_a, r_b, w_a, w_b = fields(i // hb)
        q_a, q_b, v_a, v_b = fields(pairs - 1 - i // hb)
        upper = eliminate(i, r_a, w_a, upper)
        lower = eliminate(every - 1 - i, q_b, v_b, lower)
        upper = eliminate(i + 1, r_b, w_b, upper)
        lower = eliminate(every - 2 - i, q_a, v_a, lower)
    top, low_t = half - 1, half
    joint = 1.0 / (1.0 - rat[top] * rat[low_t])

    def outward(ref):
        a = (ref[top] - rat[top] * ref[low_t]) * joint
        b = ref[low_t] - rat[low_t] * a
        ref[top], ref[low_t] = a, b
        for i in range(1, half):
            a = ref[top - i] - rat[top - i] * a
            b = ref[low_t + i] - rat[low_t + i] * b
            ref[top - i], ref[low_t + i] = a, b

    def inward(source, ref):
        a = b = None
        for i in range(half):
            j = every - 1 - i
            a = source[i] * inv[i] if a is None else source[i] * inv[i] - rat[i] * a
            b = source[j] * inv[j] if b is None else source[j] * inv[j] - rat[j] * b
            ref[i], ref[j] = a, b

    last, initial = sub == SUB - 1, sub == 0
    edge = (last & ~low) | (initial & low)
    low_row = low[:1]

    def beside(v, t, base):
        across = jnp.where(edge, turn(v, HALF), 0.0)
        line = jnp.where(low_row, across[:1], across[SUB - 1 :])
        pair, h = divmod(t, hb)
        side[pair, base + 1 + h : base + 2 + h] = line
        other, spot = (pair - 1, hb + 1) if h == 0 else (pair + 1, 0)
        if 0 <= other < pairs:
            side[other, base + spot : base + spot + 1] = line
        up = pltpu.roll(jnp.where(last, across, v), 1, 0)
        down = pltpu.roll(jnp.where(initial, across, v), SUB - 1, 0)
        return (up + down) + (turn(v, 1) + turn(v, -1))

    def split(ref, result, base):
        old, now = zero, beside(ref[0], 0, base)
        for t in range(every):
            new = beside(ref[t + 1], t + 1, base) if t + 1 < every else zero
            value = hour_weight(t) * now - coupling * (old + new)
            result[t] = jnp.where(inside, value, 0.0)
            old, now = now, new

    side[0], side[pairs - 1] = zero, zero
    outward(z0)
    split(z0, s1, 0)
    inward(s1, y1)
    outward(y1)
    split(y1, s2, hb + 2)
    inward(s2, y2)
    outward(y2)

    total = zero
    products = ((right, z0), (z0, s1), (right, y1), (s1, y1), (z0, s2), (y1, s2))
    for row, (x, y) in enumerate(products):
        parts = [x[t] * y[t] for t in range(4)]
        for t in range(4, every):
            parts[t % 4] = parts[t % 4] + x[t] * y[t]
        part = jnp.where(own, (parts[0] + parts[1]) + (parts[2] + parts[3]), 0.0)
        part = jnp.sum(part, axis=0, keepdims=True)
        total = jnp.where(sub == row, part, total)
    total = turn(total + turn(total, HALF), SLOT)

    def two(ref, pair):
        before = ref[pair * hb - 1] if pair > 0 else zero
        after = ref[pair * hb + hb] if pair + 1 < pairs else zero
        return jnp.where(first, before, turn(after, SLOT))

    for pair in range(pairs):
        groups = (
            (two(z0, pair), two(y1, pair)),
            (two(y2, pair), jnp.where(first, side[pair], total)),
        )
        for g, (a, b) in enumerate(groups):
            for strip, chunk in enumerate(halves(a, b, left)):
                out[strips * pair + strip, g] = chunk


def unpack_kernel(got, right, weight, kappa, solution, residual, precond, z0, y1, y2, side):
    blocks = got.shape[0]
    tiles = blocks // SLOTS
    hb = 2
    lane, sub = lanes_of()
    left = lane < HALF
    first = lax.rem(lane, HALF) < SLOT
    parts = [got[c, 1] for c in range(4)]
    for c in range(4, blocks):
        parts[c % 4] = parts[c % 4] + got[c, 1]
    total = (parts[0] + parts[1]) + (parts[2] + parts[3])
    total = jnp.sum(jnp.where(lane >= LANES - SLOT, total, 0.0), axis=1, keepdims=True)
    total = jnp.broadcast_to(total, (SUB, LANES))
    sums = [jnp.broadcast_to(total[i : i + 1], (SUB, LANES)) for i in range(6)]
    cx, c2, c0, c1 = step_scalars(*sums)

    for k in range(tiles):
        at = pl.ds(k * LANES, LANES)
        early, late = (
            quad([got[k * SLOTS + j, g] for j in range(SLOTS)], left, first) for g in (0, 1)
        )
        z0[0, :, at], z0[hb + 1, :, at] = early[0], early[1]
        y1[0, :, at], y1[hb + 1, :, at] = early[2], early[3]
        y2[0, :, at], y2[1, :, at] = late[0], late[1]
        side[:, at] = late[2]

    mine, strip = lax.axis_index("tm"), lax.axis_index("rows")
    inner = 1.0 + coupling * coupling
    e_a = jnp.where(mine == 0, 1.0, inner)
    e_b = jnp.where(mine == lax.axis_size("tm") - 1, 1.0, inner)
    last, initial = sub == SUB - 1, sub == 0
    edge = (sub == jnp.where(strip == 0, 0, SUB - 1))

    def block_solve(k, f_a, f_b, before, after):
        diag = tile(kappa, k) + 4.0
        off = -coupling * diag
        d_a = e_a * diag + tile(weight, k, 0)
        d_b = e_b * diag + tile(weight, k, 1)
        scale = 1.0 / (d_a * d_b - off * off)
        f_a, f_b = f_a - off * before, f_b - off * after
        return (d_b * f_a - off * f_b) * scale, (d_a * f_b - off * f_a) * scale

    def split(ref, base):
        forward = [[turn(tile(ref, k, q), 1) for k in range(tiles)] for q in range(hb + 2)]
        back = [[turn(tile(ref, k, q), -1) for k in range(tiles)] for q in range(hb + 2)]
        result = []
        for k in range(tiles):
            near = []
            for q in range(hb + 2):
                v = tile(ref, k, q)
                line = side[base + q : base + q + 1, pl.ds(k * LANES, LANES)]
                across = jnp.where(edge, line, 0.0)
                up = pltpu.roll(jnp.where(last, across, v), 1, 0)
                down = pltpu.roll(jnp.where(initial, across, v), SUB - 1, 0)
                west = jnp.where(lane == 0, forward[q][k - 1] if k else 0.0, forward[q][k])
                east = back[q][k + 1] if k + 1 < tiles else 0.0
                east = jnp.where(lane == LANES - 1, east, back[q][k])
                near.append((up + down) + (east + west))
            result.append(
                (
                    e_a * near[1] - coupling * (near[0] + near[2]),
                    e_b * near[2] - coupling * (near[1] + near[3]),
                )
            )
        return result

    for k in range(tiles):
        at = pl.ds(k * LANES, LANES)
        z0[1, :, at], z0[2, :, at] = block_solve(
            k, tile(right, k, 0), tile(right, k, 1), tile(z0, k, 0), tile(z0, k, 3)
        )
    s1 = split(z0, 0)
    for k in range(tiles):
        at = pl.ds(k * LANES, LANES)
        pair = block_solve(k, *s1[k], tile(y1, k, 0), tile(y1, k, 3))
        for h in range(hb):
            y1[h + 1, :, at] = pair[h]
            solution[h, :, at] = cx * tile(z0, k, h + 1) + c2 * pair[h]
            residual[h, :, at] = c0 * tile(right, k, h) + c1 * s1[k][h]
    s2 = split(y1, hb + 2)
    for k in range(tiles):
        at = pl.ds(k * LANES, LANES)
        pair = block_solve(k, *s2[k], tile(y2, k, 0), tile(y2, k, 1))
        for h in range(hb):
            residual[h, :, at] = tile(residual, k, h) + c2 * s2[k][h]
            precond[h, :, at] = (
                c0 * tile(z0, k, h + 1) + c1 * tile(y1, k, h + 1) + c2 * pair[h]
            )


def exchange(chunks, blocks):
    rows = chunks.shape[0] // blocks
    chunks = chunks.reshape(blocks, rows // EXTRA, EXTRA, LANES)
    return lax.all_to_all(chunks, AXES, split_axis=0, concat_axis=0, tiled=True).reshape(-1, LANES)


def per_device(observations, obs_noise, prior_noise, observed, kappa_sq, obs_precision):
    hours, rows, columns = observations.shape
    pairs = lax.axis_size("tm")
    blocks = pairs * lax.axis_size("rows")
    fits = (
        lax.axis_size("rows") == 2
        and hours == 2
        and rows == SUB
        and columns == blocks * SLOT
        and pairs >= SUB
        and pairs % 2 == 0
    )
    args = (observations, obs_noise, prior_noise, observed, kappa_sq, obs_precision)
    if not fits:
        return per_device_any(*args)

    def shaped(*shape):
        return jax.ShapeDtypeStruct(shape, jnp.float32)

    def room(*shape):
        return pltpu.VMEM(shape, jnp.float32)

    field = shaped(hours, rows, columns)
    right, weight, chunks = pl.pallas_call(
        pack_kernel,
        out_shape=(field, field, shaped(blocks * (rows + EXTRA), LANES)),
        name="pack",
    )(*args)
    got = exchange(chunks, blocks)
    chunks = pl.pallas_call(
        lambda *refs: solve_kernel(columns, *refs),
        out_shape=shaped(blocks, 2, rows, LANES),
        scratch_shapes=[room(pairs * hours, rows, LANES)] * 8 + [room(pairs, rows, LANES)],
        name="solve",
    )(got)
    got = lax.all_to_all(chunks, AXES, split_axis=0, concat_axis=0, tiled=True)
    return tuple(
        pl.pallas_call(
            unpack_kernel,
            out_shape=[field] * 3,
            scratch_shapes=[room(hours + 2, rows, columns)] * 2
            + [room(2, rows, columns), room(rows, columns)],
            name="unpack",
        )(got, right, weight, kappa_sq)
    )


def solution(mesh):
    whole, plane = P("tm", "rows", None), P("rows", None)
    return jax.shard_map(
        per_device,
        mesh=mesh,
        in_specs=(whole, whole, whole, whole, plane, plane),
        out_specs=(whole, whole, whole),
        check_vma=False,
    )
```

```python
import jax
import jax.numpy as jnp
from jax import lax
from jax.experimental import pallas as pl
from jax.experimental.pallas import tpu as pltpu
from jax.sharding import PartitionSpec as P

ITERS = 2
coupling = 0.995
AXES = ("tm", "rows")


def column_windows(field, blocks, halo):
    width = field.shape[-1] // blocks
    split = field.shape[:-1] + (blocks, width)
    parts = []
    for step in range(halo, 0, -1):
        moved = jnp.pad(field, [(0, 0)] * (field.ndim - 1) + [(step, 0)])[..., : field.shape[-1]]
        parts.append(moved.reshape(split)[..., :1])
    parts.append(field.reshape(split))
    for step in range(1, halo + 1):
        moved = jnp.pad(field, [(0, 0)] * (field.ndim - 1) + [(0, step)])[..., step:]
        parts.append(moved.reshape(split)[..., -1:])
    return jnp.concatenate(parts, axis=-1)


def hour_factors(main, off):
    def advance(inverse, row):
        inverse = 1.0 / (row - off * off * inverse)
        return inverse, inverse

    return lax.scan(advance, jnp.zeros_like(off), main)[1]


def hour_solve(right, inverse, ratio):
    def down(before, entries):
        value, inv, rat = entries
        now = value * inv - rat * before
        return now, now

    def up(after, entries):
        value, rat = entries
        now = value - rat * after
        return now, now

    zero = jnp.zeros_like(right[0])
    forward = lax.scan(down, zero, (right, inverse, ratio))[1]
    return lax.scan(up, zero, (forward, ratio), reverse=True)[1]


def split_off(field, weights):
    padded = jnp.pad(field, ((0, 0), (1, 1), (1, 1)))
    beside = padded[:, 2:, 1:-1] + padded[:, :-2, 1:-1] + padded[:, 1:-1, 2:] + padded[:, 1:-1, :-2]
    hours = jnp.pad(beside, ((1, 1), (0, 0), (0, 0)))
    return weights * beside - coupling * (hours[2:] + hours[:-2])


def step_scalars(a, h, hp, k, m, n):
    alpha = a / (a - h)
    delta = -h / (a - h)
    rz = delta * delta * a + alpha * delta * (h + hp) + alpha * alpha * k
    g = delta + rz / a
    curve = g * g * (a - h) + g * alpha * (h - m + hp - k) + alpha * alpha * (k - n)
    beta = rz / curve
    return alpha + beta * g, beta * alpha, delta - beta * g, alpha + beta * g - beta * alpha


def per_device_any(observations, obs_noise, prior_noise, observed, kappa_sq, obs_precision):
    hours, rows, columns = observations.shape
    over_tm, over_rows = lax.axis_size("tm"), lax.axis_size("rows")
    blocks = over_tm * over_rows
    width = columns // blocks
    wide = width + 2 * ITERS
    mask = observed.astype(jnp.float32)
    obs_weight = mask * obs_precision
    right = (
        mask * (obs_precision * observations + jnp.sqrt(obs_precision) * obs_noise) + prior_noise
    )
    payload = jnp.concatenate([right, obs_weight, kappa_sq[None]], axis=0)
    payload = jnp.moveaxis(column_windows(payload, blocks, ITERS), 2, 0)
    payload = payload.reshape(blocks, -1)
    got = lax.all_to_all(payload, AXES, split_axis=0, concat_axis=0, tiled=True)
    got = got.reshape(over_tm, over_rows, 2 * hours + 1, rows, wide)
    got = jnp.moveaxis(got, 2, 1)
    all_rows = over_rows * rows
    every = over_tm * hours
    r0 = got[:, :hours].reshape(every, all_rows, wide)
    ow = got[:, hours : 2 * hours].reshape(every, all_rows, wide)
    diag = got[0, 2 * hours].reshape(all_rows, wide) + 4.0
    where = (lax.axis_index("tm") * over_rows + lax.axis_index("rows")) * width
    column = where - ITERS + jnp.arange(wide, dtype=jnp.int32)
    inside = (column >= 0) & (column < columns)
    hour = jnp.arange(every)
    ends = (hour == 0) | (hour == every - 1)
    weights = jnp.where(ends, 1.0, 1.0 + coupling * coupling).astype(jnp.float32)[:, None, None]
    off = -coupling * diag
    inverse = hour_factors(weights * diag + ow, off)
    ratio = off * inverse
    z0 = hour_solve(r0, inverse, ratio)
    s1 = jnp.where(inside, split_off(z0, weights), 0.0)
    y1 = hour_solve(s1, inverse, ratio)
    s2 = jnp.where(inside, split_off(y1, weights), 0.0)
    y2 = hour_solve(s2, inverse, ratio)
    own = slice(ITERS, ITERS + width)
    r0, z0, s1, y1, s2, y2 = (part[:, :, own] for part in (r0, z0, s1, y1, s2, y2))
    pairs = ((r0, z0), (z0, s1), (r0, y1), (s1, y1), (z0, s2), (y1, s2))
    sums = jnp.stack([jnp.sum(x * y) for x, y in pairs])
    back = jnp.stack([z0, y1, y2, s1, s2]).reshape(-1, over_tm, hours, over_rows, rows, width)
    items = back.shape[0]
    back = back.transpose(1, 3, 0, 2, 4, 5).reshape(blocks, -1)
    back = jnp.concatenate([back, jnp.broadcast_to(sums, (blocks, sums.shape[0]))], axis=1)
    got = lax.all_to_all(back, AXES, split_axis=0, concat_axis=0, tiled=True)
    sums = jnp.sum(got[:, -sums.shape[0] :], axis=0)
    got = got[:, : -sums.shape[0]].reshape(blocks, items, hours, rows, width)
    z0, y1, y2, s1, s2 = got.transpose(1, 2, 3, 0, 4).reshape(items, hours, rows, columns)
    cx, c2, c0, c1 = step_scalars(*sums)
    return (
        cx * z0 + c2 * y1,
        c0 * right + c1 * s1 + c2 * s2,
        c0 * z0 + c1 * y1 + c2 * y2,
    )


LANES, SUB = 128, 8
HALF = LANES // 2
SLOTS = 4
SLOT = LANES // SLOTS
EXTRA = 2


def lanes_of():
    lane = lax.broadcasted_iota(jnp.int32, (SUB, LANES), 1)
    sub = lax.broadcasted_iota(jnp.int32, (SUB, LANES), 0)
    return lane, sub


def turn(x, shift):
    shift = shift % LANES
    return x if shift == 0 else pltpu.roll(x, shift, 1)


def halves(a, b, left):
    return jnp.where(left, a, turn(b, HALF)), jnp.where(left, turn(a, HALF), b)


def quad(q, left, first):
    p0, p2 = halves(q[0], q[2], left)
    p1, p3 = halves(q[1], q[3], left)
    result = []
    for a, b in ((p0, p1), (p2, p3)):
        result.append(jnp.where(first, a, turn(b, SLOT)))
        result.append(jnp.where(first, turn(a, -SLOT), b))
    return result


def tile(ref, k, *row):
    at = pl.ds(k * LANES, LANES)
    return ref[row + (slice(None), at)] if row else ref[:, at]


def pack_kernel(obs, noise, prior, observed, kappa, precision, right, weight, out):
    hours, _, columns = obs.shape
    tiles = columns // LANES
    blocks = tiles * SLOTS
    lane, sub = lanes_of()
    left = lane < HALF
    slot_lane = lax.rem(lane, SLOT)
    first = lax.rem(lane, HALF) < SLOT
    rows = SUB + EXTRA
    prec = precision[...]
    root = jnp.sqrt(prec)
    for h in range(hours):
        mask = observed[h].astype(jnp.float32)
        right[h] = mask * (prec * obs[h] + root * noise[h]) + prior[h]
        weight[h] = mask * prec
    zero = jnp.zeros((SUB, LANES), jnp.float32)

    span = 2 * ITERS
    beginnings, endings = [], []
    for k in range(tiles):
        items = [tile(ref, k, h) for ref in (right, weight) for h in range(hours)]
        for j, chunk in enumerate(quad(items, left, first)):
            out[pl.ds((k * SLOTS + j) * rows, SUB), :] = chunk
        begin, end = zero, zero
        for i, item in enumerate(items):
            at = i * span
            begin = jnp.where(slot_lane // ITERS == i * 2 + 1, turn(item, at + ITERS), begin)
            end = jnp.where(slot_lane // ITERS == i * 2, turn(item, at - SLOT + ITERS), end)
        falling = lax.rem(SUB - sub, SUB)
        beginnings.append(jnp.take_along_axis(begin, falling, axis=0))
        endings.append(jnp.take_along_axis(end, falling, axis=0))

    line = lax.rem(lax.axis_index("tm"), SUB)
    kap = [
        jnp.sum(jnp.where(sub == line, tile(kappa, k), 0.0), axis=0, keepdims=True)
        for k in range(tiles)
    ]
    wide = len(items) * span
    before = lax.rem(lane // ITERS, 2) == 0
    lane_row = lax.broadcasted_iota(jnp.int32, (1, LANES), 1)
    for block in range(blocks):
        k, j = divmod(block, SLOTS)
        at = j * SLOT
        prev = turn(endings[(block - 1) // SLOTS], SLOT - at) if block else zero
        last = block == blocks - 1
        follow = zero if last else turn(beginnings[(block + 1) // SLOTS], -at - SLOT)
        halo = jnp.where(lane < wide, jnp.where(before, prev, follow), 0.0)
        halo = pltpu.roll(halo, 0, 1, stride=wide, stride_axis=0)
        out[pl.ds(block * rows + SUB, 1), :] = jnp.sum(halo, axis=0, keepdims=True)
        here = kap[k]
        if j == 0 and k > 0:
            here = jnp.where(lane_row >= HALF, kap[k - 1], here)
        if j == SLOTS - 1 and k + 1 < tiles:
            here = jnp.where(lane_row < HALF, kap[k + 1], here)
        out[pl.ds(block * rows + SUB + 1, 1), :] = turn(here, -at)


def solve_kernel(columns, got, out, right, inv, rat, z0, y1, y2, s1, s2, side):
    strips, hb = 2, 2
    rows = SUB + EXTRA
    blocks = got.shape[0] // rows
    pairs = blocks // strips
    every = pairs * hb
    width = SLOT
    half = every // 2
    lane, sub = lanes_of()
    left = lane < HALF
    first = lax.rem(lane, HALF) < SLOT
    low = lax.rem(lane + ITERS, LANES) < HALF
    place = lax.rem(lane + ITERS, HALF) - ITERS
    block = lax.axis_index("tm") * strips + lax.axis_index("rows")
    column = block * width + place
    window = place < width + ITERS
    inside = window & (column >= 0) & (column < columns)
    own = (place >= 0) & (place < width)
    ahead = place < 0
    zero = jnp.zeros((SUB, LANES), jnp.float32)

    def strip_rows(at):
        return [jnp.broadcast_to(got[pl.ds(at + s * rows, 1), :], (SUB, LANES)) for s in (0, 1)]

    kap = [zero, zero]
    for i in range(SUB):
        lines = strip_rows(i * strips * rows + SUB + 1)
        kap = [jnp.where(sub == i, line, k) for line, k in zip(lines, kap)]
    kap = jnp.where(low, kap[0], turn(kap[1], HALF))
    diag = jnp.where(window, kap, 0.0) + 4.0
    off = -coupling * diag
    off_sq = off * off
    inner = (1.0 + coupling * coupling) * diag

    span = 2 * ITERS
    wide = 2 * hb * span

    def fields(pair):
        at = pair * strips * rows
        c0, c1 = got[pl.ds(at, SUB), :], got[pl.ds(at + rows, SUB), :]
        h0, h1 = (
            pltpu.roll(line, 0, 1, stride=wide, stride_axis=0)
            for line in strip_rows(at + SUB)
        )
        halo = jnp.where(left, h0, turn(h1, HALF))
        result = []
        for i, mine in enumerate(halves(c0, c1, left)):
            for h in range(hb):
                item = i * hb + h
                around = jnp.where(
                    ahead,
                    turn(halo, -ITERS - item * span),
                    turn(halo, SLOT - ITERS - item * span),
                )
                result.append(jnp.where(own, turn(mine, -h * SLOT), around))
        return result

    def hour_weight(t):
        return 1.0 if t in (0, every - 1) else 1.0 + coupling * coupling

    def eliminate(t, rhs, weight, before):
        main = jnp.where(window, weight, 0.0) + (diag if t in (0, every - 1) else inner)
        pivot = main if before is None else main - off_sq * before[0]
        iv = 1.0 / pivot
        c = off * iv
        g = rhs * iv if before is None else rhs * iv - c * before[1]
        right[t], inv[t], rat[t], z0[t] = rhs, iv, c, g
        return iv, g

    upper = lower = None
    for i in range(0, half, hb):
        r_a, r_b, w_a, w_b = fields(i // hb)
        q_a, q_b, v_a, v_b = fields(pairs - 1 - i // hb)
        upper = eliminate(i, r_a, w_a, upper)
        lower = eliminate(every - 1 - i, q_b, v_b, lower)
        upper = eliminate(i + 1, r_b, w_b, upper)
        lower = eliminate(every - 2 - i, q_a, v_a, lower)
    top, low_t = half - 1, half
    joint = 1.0 / (1.0 - rat[top] * rat[low_t])

    def outward(ref):
        a = (ref[top] - rat[top] * ref[low_t]) * joint
        b = ref[low_t] - rat[low_t] * a
        ref[top], ref[low_t] = a, b
        for i in range(1, half):
            a = ref[top - i] - rat[top - i] * a
            b = ref[low_t + i] - rat[low_t + i] * b
            ref[top - i], ref[low_t + i] = a, b

    def inward(source, ref):
        a = b = None
        for i in range(half):
            j = every - 1 - i
            a = source[i] * inv[i] if a is None else source[i] * inv[i] - rat[i] * a
            b = source[j] * inv[j] if b is None else source[j] * inv[j] - rat[j] * b
            ref[i], ref[j] = a, b

    last, initial = sub == SUB - 1, sub == 0
    edge = (last & ~low) | (initial & low)
    low_row = low[:1]

    def beside(v, t, base):
        across = jnp.where(edge, turn(v, HALF), 0.0)
        line = jnp.where(low_row, across[:1], across[SUB - 1 :])
        pair, h = divmod(t, hb)
        side[pair, base + 1 + h : base + 2 + h] = line
        other, spot = (pair - 1, hb + 1) if h == 0 else (pair + 1, 0)
        if 0 <= other < pairs:
            side[other, base + spot : base + spot + 1] = line
        up = pltpu.roll(jnp.where(last, across, v), 1, 0)
        down = pltpu.roll(jnp.where(initial, across, v), SUB - 1, 0)
        return (up + down) + (turn(v, 1) + turn(v, -1))

    def split(ref, result, base):
        old, now = zero, beside(ref[0], 0, base)
        for t in range(every):
            new = beside(ref[t + 1], t + 1, base) if t + 1 < every else zero
            value = hour_weight(t) * now - coupling * (old + new)
            result[t] = jnp.where(inside, value, 0.0)
            old, now = now, new

    side[0], side[pairs - 1] = zero, zero
    outward(z0)
    split(z0, s1, 0)
    inward(s1, y1)
    outward(y1)
    split(y1, s2, hb + 2)
    inward(s2, y2)
    outward(y2)

    total = zero
    products = ((right, z0), (z0, s1), (right, y1), (s1, y1), (z0, s2), (y1, s2))
    for row, (x, y) in enumerate(products):
        parts = [x[t] * y[t] for t in range(4)]
        for t in range(4, every):
            parts[t % 4] = parts[t % 4] + x[t] * y[t]
        part = jnp.where(own, (parts[0] + parts[1]) + (parts[2] + parts[3]), 0.0)
        part = jnp.sum(part, axis=0, keepdims=True)
        total = jnp.where(sub == row, part, total)
    total = turn(total + turn(total, HALF), SLOT)

    def two(ref, pair):
        before = ref[pair * hb - 1] if pair > 0 else zero
        after = ref[pair * hb + hb] if pair + 1 < pairs else zero
        return jnp.where(first, before, turn(after, SLOT))

    for pair in range(pairs):
        groups = (
            (two(z0, pair), two(y1, pair)),
            (two(y2, pair), jnp.where(first, side[pair], total)),
        )
        for g, (a, b) in enumerate(groups):
            for strip, chunk in enumerate(halves(a, b, left)):
                out[strips * pair + strip, g] = chunk


def unpack_kernel(got, right, weight, kappa, solution, residual, precond, z0, y1, y2, side):
    blocks = got.shape[0]
    tiles = blocks // SLOTS
    hb = 2
    lane, sub = lanes_of()
    left = lane < HALF
    first = lax.rem(lane, HALF) < SLOT
    parts = [got[c, 1] for c in range(4)]
    for c in range(4, blocks):
        parts[c % 4] = parts[c % 4] + got[c, 1]
    total = (parts[0] + parts[1]) + (parts[2] + parts[3])
    total = jnp.sum(jnp.where(lane >= LANES - SLOT, total, 0.0), axis=1, keepdims=True)
    total = jnp.broadcast_to(total, (SUB, LANES))
    sums = [jnp.broadcast_to(total[i : i + 1], (SUB, LANES)) for i in range(6)]
    cx, c2, c0, c1 = step_scalars(*sums)

    for k in range(tiles):
        at = pl.ds(k * LANES, LANES)
        early, late = (
            quad([got[k * SLOTS + j, g] for j in range(SLOTS)], left, first) for g in (0, 1)
        )
        z0[0, :, at], z0[hb + 1, :, at] = early[0], early[1]
        y1[0, :, at], y1[hb + 1, :, at] = early[2], early[3]
        y2[0, :, at], y2[1, :, at] = late[0], late[1]
        side[:, at] = late[2]

    mine, strip = lax.axis_index("tm"), lax.axis_index("rows")
    inner = 1.0 + coupling * coupling
    e_a = jnp.where(mine == 0, 1.0, inner)
    e_b = jnp.where(mine == lax.axis_size("tm") - 1, 1.0, inner)
    last, initial = sub == SUB - 1, sub == 0
    edge = (sub == jnp.where(strip == 0, 0, SUB - 1))

    def block_solve(k, f_a, f_b, before, after):
        diag = tile(kappa, k) + 4.0
        off = -coupling * diag
        d_a = e_a * diag + tile(weight, k, 0)
        d_b = e_b * diag + tile(weight, k, 1)
        scale = 1.0 / (d_a * d_b - off * off)
        f_a, f_b = f_a - off * before, f_b - off * after
        return (d_b * f_a - off * f_b) * scale, (d_a * f_b - off * f_a) * scale

    def split(ref, base):
        forward = [[turn(tile(ref, k, q), 1) for k in range(tiles)] for q in range(hb + 2)]
        back = [[turn(tile(ref, k, q), -1) for k in range(tiles)] for q in range(hb + 2)]
        result = []
        for k in range(tiles):
            near = []
            for q in range(hb + 2):
                v = tile(ref, k, q)
                line = side[base + q : base + q + 1, pl.ds(k * LANES, LANES)]
                across = jnp.where(edge, line, 0.0)
                up = pltpu.roll(jnp.where(last, across, v), 1, 0)
                down = pltpu.roll(jnp.where(initial, across, v), SUB - 1, 0)
                west = jnp.where(lane == 0, forward[q][k - 1] if k else 0.0, forward[q][k])
                east = back[q][k + 1] if k + 1 < tiles else 0.0
                east = jnp.where(lane == LANES - 1, east, back[q][k])
                near.append((up + down) + (east + west))
            result.append(
                (
                    e_a * near[1] - coupling * (near[0] + near[2]),
                    e_b * near[2] - coupling * (near[1] + near[3]),
                )
            )
        return result

    for k in range(tiles):
        at = pl.ds(k * LANES, LANES)
        z0[1, :, at], z0[2, :, at] = block_solve(
            k, tile(right, k, 0), tile(right, k, 1), tile(z0, k, 0), tile(z0, k, 3)
        )
    s1 = split(z0, 0)
    for k in range(tiles):
        at = pl.ds(k * LANES, LANES)
        pair = block_solve(k, *s1[k], tile(y1, k, 0), tile(y1, k, 3))
        for h in range(hb):
            y1[h + 1, :, at] = pair[h]
            solution[h, :, at] = cx * tile(z0, k, h + 1) + c2 * pair[h]
            residual[h, :, at] = c0 * tile(right, k, h) + c1 * s1[k][h]
    s2 = split(y1, hb + 2)
    for k in range(tiles):
        at = pl.ds(k * LANES, LANES)
        pair = block_solve(k, *s2[k], tile(y2, k, 0), tile(y2, k, 1))
        for h in range(hb):
            residual[h, :, at] = tile(residual, k, h) + c2 * s2[k][h]
            precond[h, :, at] = (
                c0 * tile(z0, k, h + 1) + c1 * tile(y1, k, h + 1) + c2 * pair[h]
            )


def exchange(chunks, blocks):
    rows = chunks.shape[0] // blocks
    chunks = chunks.reshape(blocks, rows // EXTRA, EXTRA, LANES)
    return lax.all_to_all(chunks, AXES, split_axis=0, concat_axis=0, tiled=True).reshape(-1, LANES)


def per_device(observations, obs_noise, prior_noise, observed, kappa_sq, obs_precision):
    hours, rows, columns = observations.shape
    pairs = lax.axis_size("tm")
    blocks = pairs * lax.axis_size("rows")
    fits = (
        lax.axis_size("rows") == 2
        and hours == 2
        and rows == SUB
        and columns == blocks * SLOT
        and pairs >= SUB
        and pairs % 2 == 0
    )
    args = (observations, obs_noise, prior_noise, observed, kappa_sq, obs_precision)
    if not fits:
        return per_device_any(*args)

    def shaped(*shape):
        return jax.ShapeDtypeStruct(shape, jnp.float32)

    def room(*shape):
        return pltpu.VMEM(shape, jnp.float32)

    field = shaped(hours, rows, columns)
    right, weight, chunks = pl.pallas_call(
        pack_kernel,
        out_shape=(
            pltpu.VMEM((hours, rows, columns), jnp.float32),
            pltpu.VMEM((hours, rows, columns), jnp.float32),
            pltpu.VMEM((blocks * (rows + EXTRA), LANES), jnp.float32),
        ),
        name="pack",
    )(*args)
    got = exchange(chunks, blocks)
    chunks = pl.pallas_call(
        lambda *refs: solve_kernel(columns, *refs),
        out_shape=pltpu.VMEM((blocks, 2, rows, LANES), jnp.float32),
        scratch_shapes=[room(pairs * hours, rows, LANES)] * 8 + [room(pairs, rows, LANES)],
        name="solve",
    )(pltpu.with_memory_space_constraint(got, pltpu.VMEM))
    got = lax.all_to_all(chunks, AXES, split_axis=0, concat_axis=0, tiled=True)
    return tuple(
        pl.pallas_call(
            unpack_kernel,
            out_shape=[field] * 3,
            scratch_shapes=[room(hours + 2, rows, columns)] * 2
            + [room(2, rows, columns), room(rows, columns)],
            name="unpack",
        )(*(pltpu.with_memory_space_constraint(x, pltpu.VMEM) for x in (got, right, weight, kappa_sq)))
    )


def solution(mesh):
    whole, plane = P("tm", "rows", None), P("rows", None)
    return jax.shard_map(
        per_device,
        mesh=mesh,
        in_specs=(whole, whole, whole, whole, plane, plane),
        out_specs=(whole, whole, whole),
        check_vma=False,
    )
```

```python
import jax
import jax.numpy as jnp
from jax import lax
from jax.experimental import pallas as pl
from jax.experimental.pallas import tpu as pltpu
from jax.sharding import PartitionSpec as P

ITERS = 2
coupling = 0.995
AXES = ("tm", "rows")


def column_windows(field, blocks, halo):
    width = field.shape[-1] // blocks
    split = field.shape[:-1] + (blocks, width)
    parts = []
    for step in range(halo, 0, -1):
        moved = jnp.pad(field, [(0, 0)] * (field.ndim - 1) + [(step, 0)])[..., : field.shape[-1]]
        parts.append(moved.reshape(split)[..., :1])
    parts.append(field.reshape(split))
    for step in range(1, halo + 1):
        moved = jnp.pad(field, [(0, 0)] * (field.ndim - 1) + [(0, step)])[..., step:]
        parts.append(moved.reshape(split)[..., -1:])
    return jnp.concatenate(parts, axis=-1)


def hour_factors(main, off):
    def advance(inverse, row):
        inverse = 1.0 / (row - off * off * inverse)
        return inverse, inverse

    return lax.scan(advance, jnp.zeros_like(off), main)[1]


def hour_solve(right, inverse, ratio):
    def down(before, entries):
        value, inv, rat = entries
        now = value * inv - rat * before
        return now, now

    def up(after, entries):
        value, rat = entries
        now = value - rat * after
        return now, now

    zero = jnp.zeros_like(right[0])
    forward = lax.scan(down, zero, (right, inverse, ratio))[1]
    return lax.scan(up, zero, (forward, ratio), reverse=True)[1]


def split_off(field, weights):
    padded = jnp.pad(field, ((0, 0), (1, 1), (1, 1)))
    beside = padded[:, 2:, 1:-1] + padded[:, :-2, 1:-1] + padded[:, 1:-1, 2:] + padded[:, 1:-1, :-2]
    hours = jnp.pad(beside, ((1, 1), (0, 0), (0, 0)))
    return weights * beside - coupling * (hours[2:] + hours[:-2])


def step_scalars(a, h, hp, k, m, n):
    alpha = a / (a - h)
    delta = -h / (a - h)
    rz = delta * delta * a + alpha * delta * (h + hp) + alpha * alpha * k
    g = delta + rz / a
    curve = g * g * (a - h) + g * alpha * (h - m + hp - k) + alpha * alpha * (k - n)
    beta = rz / curve
    return alpha + beta * g, beta * alpha, delta - beta * g, alpha + beta * g - beta * alpha


def per_device_any(observations, obs_noise, prior_noise, observed, kappa_sq, obs_precision):
    hours, rows, columns = observations.shape
    over_tm, over_rows = lax.axis_size("tm"), lax.axis_size("rows")
    blocks = over_tm * over_rows
    width = columns // blocks
    wide = width + 2 * ITERS
    mask = observed.astype(jnp.float32)
    obs_weight = mask * obs_precision
    right = (
        mask * (obs_precision * observations + jnp.sqrt(obs_precision) * obs_noise) + prior_noise
    )
    payload = jnp.concatenate([right, obs_weight, kappa_sq[None]], axis=0)
    payload = jnp.moveaxis(column_windows(payload, blocks, ITERS), 2, 0)
    payload = payload.reshape(blocks, -1)
    got = lax.all_to_all(payload, AXES, split_axis=0, concat_axis=0, tiled=True)
    got = got.reshape(over_tm, over_rows, 2 * hours + 1, rows, wide)
    got = jnp.moveaxis(got, 2, 1)
    all_rows = over_rows * rows
    every = over_tm * hours
    r0 = got[:, :hours].reshape(every, all_rows, wide)
    ow = got[:, hours : 2 * hours].reshape(every, all_rows, wide)
    diag = got[0, 2 * hours].reshape(all_rows, wide) + 4.0
    where = (lax.axis_index("tm") * over_rows + lax.axis_index("rows")) * width
    column = where - ITERS + jnp.arange(wide, dtype=jnp.int32)
    inside = (column >= 0) & (column < columns)
    hour = jnp.arange(every)
    ends = (hour == 0) | (hour == every - 1)
    weights = jnp.where(ends, 1.0, 1.0 + coupling * coupling).astype(jnp.float32)[:, None, None]
    off = -coupling * diag
    inverse = hour_factors(weights * diag + ow, off)
    ratio = off * inverse
    z0 = hour_solve(r0, inverse, ratio)
    s1 = jnp.where(inside, split_off(z0, weights), 0.0)
    y1 = hour_solve(s1, inverse, ratio)
    s2 = jnp.where(inside, split_off(y1, weights), 0.0)
    y2 = hour_solve(s2, inverse, ratio)
    own = slice(ITERS, ITERS + width)
    r0, z0, s1, y1, s2, y2 = (part[:, :, own] for part in (r0, z0, s1, y1, s2, y2))
    pairs = ((r0, z0), (z0, s1), (r0, y1), (s1, y1), (z0, s2), (y1, s2))
    sums = jnp.stack([jnp.sum(x * y) for x, y in pairs])
    back = jnp.stack([z0, y1, y2, s1, s2]).reshape(-1, over_tm, hours, over_rows, rows, width)
    items = back.shape[0]
    back = back.transpose(1, 3, 0, 2, 4, 5).reshape(blocks, -1)
    back = jnp.concatenate([back, jnp.broadcast_to(sums, (blocks, sums.shape[0]))], axis=1)
    got = lax.all_to_all(back, AXES, split_axis=0, concat_axis=0, tiled=True)
    sums = jnp.sum(got[:, -sums.shape[0] :], axis=0)
    got = got[:, : -sums.shape[0]].reshape(blocks, items, hours, rows, width)
    z0, y1, y2, s1, s2 = got.transpose(1, 2, 3, 0, 4).reshape(items, hours, rows, columns)
    cx, c2, c0, c1 = step_scalars(*sums)
    return (
        cx * z0 + c2 * y1,
        c0 * right + c1 * s1 + c2 * s2,
        c0 * z0 + c1 * y1 + c2 * y2,
    )


LANES, SUB = 128, 8
HALF = LANES // 2
SLOTS = 4
SLOT = LANES // SLOTS
EXTRA = 2


def lanes_of():
    lane = lax.broadcasted_iota(jnp.int32, (SUB, LANES), 1)
    sub = lax.broadcasted_iota(jnp.int32, (SUB, LANES), 0)
    return lane, sub


def turn(x, shift):
    shift = shift % LANES
    return x if shift == 0 else pltpu.roll(x, shift, 1)


def halves(a, b, left):
    return jnp.where(left, a, turn(b, HALF)), jnp.where(left, turn(a, HALF), b)


def quad(q, left, first):
    p0, p2 = halves(q[0], q[2], left)
    p1, p3 = halves(q[1], q[3], left)
    result = []
    for a, b in ((p0, p1), (p2, p3)):
        result.append(jnp.where(first, a, turn(b, SLOT)))
        result.append(jnp.where(first, turn(a, -SLOT), b))
    return result


def tile(ref, k, *row):
    at = pl.ds(k * LANES, LANES)
    return ref[row + (slice(None), at)] if row else ref[:, at]


def pack_kernel(obs, noise, prior, observed, kappa, precision, right, weight, out):
    hours, _, columns = obs.shape
    tiles = columns // LANES
    blocks = tiles * SLOTS
    lane, sub = lanes_of()
    left = lane < HALF
    slot_lane = lax.rem(lane, SLOT)
    first = lax.rem(lane, HALF) < SLOT
    rows = SUB + EXTRA
    prec = precision[...]
    root = jnp.sqrt(prec)
    for h in range(hours):
        mask = observed[h].astype(jnp.float32)
        right[h] = mask * (prec * obs[h] + root * noise[h]) + prior[h]
        weight[h] = mask * prec
    zero = jnp.zeros((SUB, LANES), jnp.float32)

    span = 2 * ITERS
    wide = 2 * hours * span
    before = lax.rem(lane // ITERS, 2) == 0
    ends, begins = [], []
    for k in range(tiles):
        items = [tile(ref, k, h) for ref in (right, weight) for h in range(hours)]
        for j, chunk in enumerate(quad(items, left, first)):
            out[pl.ds((k * SLOTS + j) * rows, SUB), :] = chunk
        begin, end = zero, zero
        for i, item in enumerate(items):
            at = i * span
            begin = jnp.where(slot_lane // ITERS == i * 2 + 1, turn(item, at + ITERS), begin)
            end = jnp.where(slot_lane // ITERS == i * 2, turn(item, at - SLOT + ITERS), end)
        ends.append(turn(end, SLOT))
        begins.append(turn(begin, -SLOT))

    def before_tile(k):
        return jnp.where(lane < SLOT, ends[k - 1] if k else 0.0, ends[k])

    def after_tile(k):
        return jnp.where(
            lane >= LANES - SLOT, begins[k + 1] if k + 1 < tiles else 0.0, begins[k]
        )

    line = lax.rem(lax.axis_index("tm"), SUB)
    kap = [
        jnp.broadcast_to(
            jnp.sum(jnp.where(sub == line, tile(kappa, k), 0.0), axis=0, keepdims=True),
            (SUB, LANES),
        )
        for k in range(tiles)
    ]

    def kappa_rows(k):
        here = jnp.where((sub < 2) & (lane >= HALF), kap[max(k - 1, 0)], kap[k])
        return jnp.where(
            (sub // 2 == 1) & (lane < HALF), kap[min(k + 1, tiles - 1)], here
        )

    falling = lax.rem(SUB - sub, SUB)
    swapped = lax.rem(lane // wide + sub, SUB)
    for k in range(0, tiles, 2):
        near = [
            jnp.where(slot_lane < wide, of(k), turn(of(k + 1), wide))
            for of in (before_tile, after_tile)
        ]
        halo = jnp.where(before, near[0], pltpu.roll(near[1], SUB - 2, 0))
        halo = jnp.take_along_axis(halo, falling, axis=0)
        halo = pltpu.roll(halo, 0, 1, stride=wide, stride_axis=0)
        halo = jnp.take_along_axis(halo, swapped, axis=0)
        halo = pltpu.roll(halo, 0, 1, stride=wide, stride_axis=0)
        lines = jnp.where(
            lax.rem(sub, 2) == 0, kappa_rows(k), turn(kappa_rows(k + 1), -SLOT // 2)
        )
        lines = pltpu.roll(lines, 0, 1, stride=SLOT // 2, stride_axis=0)
        for r in range(SUB):
            group = (SUB - r) % SUB
            block = (k + group % 2) * SLOTS + group // 2
            out[pl.ds(block * rows + SUB, 1), :] = halo[r : r + 1]
            block = (k + r % 2) * SLOTS + (SLOTS - r // 2) % SLOTS
            out[pl.ds(block * rows + SUB + 1, 1), :] = lines[r : r + 1]


def solve_kernel(columns, got, out, right, inv, rat, z0, y1, y2, s1, s2, side):
    strips, hb = 2, 2
    rows = SUB + EXTRA
    blocks = got.shape[0] // rows
    pairs = blocks // strips
    every = pairs * hb
    width = SLOT
    half = every // 2
    lane, sub = lanes_of()
    left = lane < HALF
    first = lax.rem(lane, HALF) < SLOT
    low = lax.rem(lane + ITERS, LANES) < HALF
    place = lax.rem(lane + ITERS, HALF) - ITERS
    block = lax.axis_index("tm") * strips + lax.axis_index("rows")
    column = block * width + place
    window = place < width + ITERS
    inside = window & (column >= 0) & (column < columns)
    own = (place >= 0) & (place < width)
    zero = jnp.zeros((SUB, LANES), jnp.float32)

    def strip_rows(at):
        return [jnp.broadcast_to(got[pl.ds(at + s * rows, 1), :], (SUB, LANES)) for s in (0, 1)]

    kap = [zero, zero]
    for i in range(SUB):
        lines = strip_rows(i * strips * rows + SUB + 1)
        kap = [jnp.where(sub == i, line, k) for line, k in zip(lines, kap)]
    kap = jnp.where(low, kap[0], turn(kap[1], HALF))
    diag = jnp.where(window, kap, 0.0) + 4.0
    off = -coupling * diag
    off_sq = off * off
    inner = (1.0 + coupling * coupling) * diag

    span = 2 * ITERS
    wide = 2 * hb * span

    def fields(pair):
        at = pair * strips * rows
        c0, c1 = got[pl.ds(at, SUB), :], got[pl.ds(at + rows, SUB), :]
        h0, h1 = (
            pltpu.roll(line, 0, 1, stride=wide, stride_axis=0)
            for line in strip_rows(at + SUB)
        )
        halo = jnp.where(left, h0, turn(h1, HALF))
        result = []
        for i, mine in enumerate(halves(c0, c1, left)):
            for h in range(hb):
                item = i * hb + h
                around = turn(halo, -ITERS - item * span)
                result.append(jnp.where(own, turn(mine, -h * SLOT), around))
        return result

    def hour_weight(t):
        return 1.0 if t in (0, every - 1) else 1.0 + coupling * coupling

    def main_of(t, weight):
        return jnp.where(window, weight, 0.0) + (diag if t in (0, every - 1) else inner)

    def eliminate(hours, rhs, weights, before):
        main = [main_of(t, w) for t, w in zip(hours, weights)]
        pivot = main[0] if before is None else main[0] - off_sq * before[0]
        inv_a = 1.0 / pivot
        inv_b = pivot * (1.0 / (pivot * main[1] - off_sq))
        g = None if before is None else before[1]
        for t, r, iv in zip(hours, rhs, (inv_a, inv_b)):
            c = off * iv
            g = r * iv if g is None else r * iv - c * g
            right[t], inv[t], rat[t], z0[t] = r, iv, c, g
        return inv_b, g

    upper = lower = None
    for i in range(0, half, hb):
        r_a, r_b, w_a, w_b = fields(i // hb)
        q_a, q_b, v_a, v_b = fields(pairs - 1 - i // hb)
        upper = eliminate((i, i + 1), (r_a, r_b), (w_a, w_b), upper)
        lower = eliminate((every - 1 - i, every - 2 - i), (q_b, q_a), (v_b, v_a), lower)
    top, low_t = half - 1, half
    joint = 1.0 / (1.0 - rat[top] * rat[low_t])

    def outward(ref):
        a = (ref[top] - rat[top] * ref[low_t]) * joint
        b = ref[low_t] - rat[low_t] * a
        ref[top], ref[low_t] = a, b
        for i in range(1, half):
            a = ref[top - i] - rat[top - i] * a
            b = ref[low_t + i] - rat[low_t + i] * b
            ref[top - i], ref[low_t + i] = a, b

    def inward(source, ref):
        a = b = None
        for i in range(half):
            j = every - 1 - i
            a = source[i] * inv[i] if a is None else source[i] * inv[i] - rat[i] * a
            b = source[j] * inv[j] if b is None else source[j] * inv[j] - rat[j] * b
            ref[i], ref[j] = a, b

    last, initial = sub == SUB - 1, sub == 0
    edge = (last & ~low) | (initial & low)
    low_row = low[:1]

    def beside(v, t, base):
        across = jnp.where(edge, turn(v, HALF), 0.0)
        line = jnp.where(low_row, across[:1], across[SUB - 1 :])
        pair, h = divmod(t, hb)
        side[pair, base + 1 + h : base + 2 + h] = line
        other, spot = (pair - 1, hb + 1) if h == 0 else (pair + 1, 0)
        if 0 <= other < pairs:
            side[other, base + spot : base + spot + 1] = line
        up = pltpu.roll(jnp.where(last, across, v), 1, 0)
        down = pltpu.roll(jnp.where(initial, across, v), SUB - 1, 0)
        return (up + down) + (turn(v, 1) + turn(v, -1))

    def split(ref, result, base):
        old, now = zero, beside(ref[0], 0, base)
        for t in range(every):
            new = beside(ref[t + 1], t + 1, base) if t + 1 < every else zero
            value = hour_weight(t) * now - coupling * (old + new)
            result[t] = jnp.where(inside, value, 0.0)
            old, now = now, new

    side[0], side[pairs - 1] = zero, zero
    outward(z0)
    split(z0, s1, 0)
    inward(s1, y1)
    outward(y1)
    split(y1, s2, hb + 2)
    inward(s2, y2)
    outward(y2)

    totals = [zero, zero]
    products = ((right, z0), (z0, s1), (right, y1), (s1, y1), (z0, s2), (y1, s2))
    for i, (x, y) in enumerate(products):
        parts = [x[t] * y[t] for t in range(4)]
        for t in range(4, every):
            parts[t % 4] = parts[t % 4] + x[t] * y[t]
        part = jnp.where(own, (parts[0] + parts[1]) + (parts[2] + parts[3]), 0.0)
        part = jnp.sum(part, axis=0, keepdims=True)
        totals[i // 3] = jnp.where(sub == i % 3 + 2, part, totals[i // 3])
    totals = [part + turn(part, HALF) for part in totals]
    totals = [part + turn(part, -SLOT // 2) for part in totals]
    low_part = lax.rem(lane, SLOT) < SLOT // 2
    total = jnp.where(low_part, turn(totals[0], SLOT), turn(totals[1], SLOT + SLOT // 2))

    def two(ref, pair):
        before = ref[pair * hb - 1] if pair > 0 else zero
        after = ref[pair * hb + hb] if pair + 1 < pairs else zero
        return jnp.where(first, before, turn(after, SLOT))

    size = out.shape[0] // blocks
    inner_w = 1.0 + coupling * coupling
    hour_row = lax.rem(sub, hb + 2)

    def edge_rows(pair):
        lines = side[pair]
        weight = inner_w
        if pair == 0:
            weight = jnp.where(hour_row == 0, 1.0, inner_w)
        if pair == pairs - 1:
            weight = jnp.where(hour_row == 1, 1.0, inner_w)
        around = lines + pltpu.roll(lines, SUB - 2, 0)
        added = weight * pltpu.roll(lines, SUB - 1, 0) - coupling * around
        return jnp.where(sub < 4, pltpu.roll(added, 2, 0), added)

    for pair in range(pairs):
        mine = two(y2, pair)
        other = jnp.where(first, edge_rows(pair), total)
        other = jnp.where(sub >= SUB - 2, mine, other)
        for strip, chunk in enumerate(halves(pltpu.roll(mine, 2, 0), other, left)):
            out[pl.ds((strips * pair + strip) * size + SUB - 2, SUB), :] = chunk
        for strip, chunk in enumerate(halves(two(z0, pair), two(y1, pair), left)):
            out[pl.ds((strips * pair + strip) * size, SUB), :] = chunk


def at_hour(t, rows=SUB, shift=0):
    return pl.ds((t + 1) * SUB + shift, rows)


def unpack_kernel(
    got, right, weight, kappa, solution, residual, precond, z0, y1, y2, side, coef
):
    hb = 2
    size = 2 * SUB - 2
    blocks = got.shape[0] // size
    tiles = blocks // SLOTS
    lane, sub = lanes_of()
    left = lane < HALF
    first = lax.rem(lane, HALF) < SLOT
    mine, strip = lax.axis_index("tm"), lax.axis_index("rows")
    inner = 1.0 + coupling * coupling
    e_a = jnp.where(mine == 0, 1.0, inner)
    e_b = jnp.where(mine == lax.axis_size("tm") - 1, 1.0, inner)

    for k in range(tiles):
        diag = tile(kappa, k) + 4.0
        off = -coupling * diag
        d_a = e_a * diag + tile(weight, k, 0)
        d_b = e_b * diag + tile(weight, k, 1)
        scale = 1.0 / (d_a * d_b - off * off)
        coef[0, k], coef[1, k], coef[2, k], coef[3, k] = d_b * scale, off * scale, d_a * scale, off

    def early_of(c):
        return got[pl.ds(c * size, SUB), :]

    def late_of(c):
        return got[pl.ds(c * size + SUB - 2, SUB), :]

    def spot(q, k):
        return q * tiles + k

    parts = [late_of(c) for c in range(4)]
    for c in range(4, blocks):
        parts[c % 4] = parts[c % 4] + late_of(c)
    total = (parts[0] + parts[1]) + (parts[2] + parts[3])
    sums = []
    for i in range(2):
        begin = LANES - SLOT + i * (SLOT // 2)
        here = (lane >= begin) & (lane < begin + SLOT // 2)
        part = jnp.sum(jnp.where(here, total, 0.0), axis=1, keepdims=True)
        part = jnp.broadcast_to(part, (SUB, LANES))
        sums += [jnp.broadcast_to(part[r : r + 1], (SUB, LANES)) for r in range(2, 5)]
    cx, c2, c0, c1 = step_scalars(*sums)

    for k in range(tiles):
        group = range(k * SLOTS, k * SLOTS + SLOTS)
        early = quad([early_of(c) for c in group], left, first)
        for ref, b, a in ((z0, early[0], early[1]), (y1, early[2], early[3])):
            ref[at_hour(spot(0, k)), :], ref[at_hour(spot(hb + 1, k)), :] = b, a
        q = [late_of(c) for c in group]
        (p0, p2), (p1, p3) = halves(q[0], q[2], left), halves(q[1], q[3], left)
        p0, p1 = (
            jnp.where(sub < SUB - 2, pltpu.roll(p, SUB - 2, 0), high)
            for p, high in ((p0, p2), (p1, p3))
        )
        y2[0, k] = jnp.where(first, p0, turn(p1, SLOT))
        y2[1, k] = jnp.where(first, turn(p0, -SLOT), p1)
        side[k] = jnp.where(first, p2, turn(p3, SLOT))

    last, initial = sub == SUB - 1, sub == 0
    edge = sub == jnp.where(strip == 0, SUB - 1, 0)

    def block_solve(k, f_a, f_b, before, after):
        f_a, f_b = f_a - coef[3, k] * before, f_b - coef[3, k] * after
        return coef[0, k] * f_a - coef[1, k] * f_b, coef[2, k] * f_b - coef[1, k] * f_a

    quarter = range(hb + 2)

    def split(ref, base):
        passed = [0.0] * (hb + 2)
        back = [turn(ref[at_hour(spot(q, 0)), :], -1) for q in quarter]
        for k in range(tiles):
            forward = [turn(ref[at_hour(spot(q, k)), :], 1) for q in quarter]
            more = k + 1 < tiles
            coming = [
                turn(ref[at_hour(spot(q, k + 1)), :], -1) if more else 0.0 for q in quarter
            ]
            near = []
            for q in quarter:
                v = ref[at_hour(spot(q, k)), :]
                up = pltpu.roll(jnp.where(last, 0.0, v), 1, 0)
                down = pltpu.roll(jnp.where(initial, 0.0, v), SUB - 1, 0)
                west = jnp.where(lane == 0, passed[q], forward[q])
                east = jnp.where(lane == LANES - 1, coming[q], back[q])
                near.append((up + down) + (east + west))
            result = []
            for h, e in enumerate((e_a, e_b)):
                line = jnp.where(edge, side[k, base + h : base + h + 1, :], 0.0)
                result.append(e * near[h + 1] - coupling * (near[h] + near[h + 2]) + line)
            yield k, *result
            passed, back = forward, coming

    def hour(ref, q, k):
        return ref[at_hour(spot(q, k)), :]

    for k in range(tiles):
        z0[at_hour(spot(1, k)), :], z0[at_hour(spot(2, k)), :] = block_solve(
            k, tile(right, k, 0), tile(right, k, 1), hour(z0, 0, k), hour(z0, 3, k)
        )
    for k, *s1 in split(z0, 2):
        at = pl.ds(k * LANES, LANES)
        pair = block_solve(k, *s1, hour(y1, 0, k), hour(y1, 3, k))
        for h in range(hb):
            y1[at_hour(spot(h + 1, k)), :] = pair[h]
            solution[h, :, at] = cx * hour(z0, h + 1, k) + c2 * pair[h]
            residual[h, :, at] = c0 * tile(right, k, h) + c1 * s1[h]
    for k, *s2 in split(y1, 4):
        at = pl.ds(k * LANES, LANES)
        pair = block_solve(k, *s2, y2[0, k], y2[1, k])
        for h in range(hb):
            residual[h, :, at] = tile(residual, k, h) + c2 * s2[h]
            precond[h, :, at] = (
                c0 * hour(z0, h + 1, k) + c1 * hour(y1, h + 1, k) + c2 * pair[h]
            )


def exchange(chunks, blocks):
    rows = chunks.shape[0] // blocks
    chunks = chunks.reshape(blocks, rows // EXTRA, EXTRA, LANES)
    return lax.all_to_all(chunks, AXES, split_axis=0, concat_axis=0, tiled=True).reshape(-1, LANES)


def per_device(observations, obs_noise, prior_noise, observed, kappa_sq, obs_precision):
    hours, rows, columns = observations.shape
    pairs = lax.axis_size("tm")
    blocks = pairs * lax.axis_size("rows")
    fits = (
        lax.axis_size("rows") == 2
        and hours == 2
        and rows == SUB
        and columns == blocks * SLOT
        and pairs >= SUB
        and pairs % SUB == 0
    )
    args = (observations, obs_noise, prior_noise, observed, kappa_sq, obs_precision)
    if not fits:
        return per_device_any(*args)

    def shaped(*shape):
        return jax.ShapeDtypeStruct(shape, jnp.float32)

    def room(*shape):
        return pltpu.VMEM(shape, jnp.float32)

    def near(x):
        return pltpu.with_memory_space_constraint(x, pltpu.VMEM)

    field = shaped(hours, rows, columns)
    right, weight, chunks = pl.pallas_call(
        pack_kernel,
        out_shape=(
            pltpu.VMEM((hours, rows, columns), jnp.float32),
            pltpu.VMEM((hours, rows, columns), jnp.float32),
            pltpu.VMEM((blocks * (rows + EXTRA), LANES), jnp.float32),
        ),
        name="pack",
    )(*args)
    got = exchange(chunks, blocks)
    every = pairs * hours
    chunks = pl.pallas_call(
        lambda *refs: solve_kernel(columns, *refs),
        out_shape=pltpu.VMEM((blocks * (2 * rows - 2), LANES), jnp.float32),
        scratch_shapes=[room(every, rows, LANES)] * 8 + [room(pairs, rows, LANES)],
        name="solve",
    )(near(got))
    got = exchange(chunks, blocks)
    tiles = columns // LANES
    flat = room(((hours + 2) * tiles + 2) * rows, LANES)
    return tuple(
        pl.pallas_call(
            unpack_kernel,
            out_shape=[field] * 3,
            scratch_shapes=[flat] * 2
            + [room(2, tiles, rows, LANES), room(tiles, rows, LANES), room(4, tiles, rows, LANES)],
            name="unpack",
        )(*(near(x) for x in (got, right, weight, kappa_sq)))
    )


def solution(mesh):
    whole, plane = P("tm", "rows", None), P("rows", None)
    return jax.shard_map(
        per_device,
        mesh=mesh,
        in_specs=(whole, whole, whole, whole, plane, plane),
        out_specs=(whole, whole, whole),
        check_vma=False,
    )
```

```python
import jax
import jax.numpy as jnp
from jax import lax
from jax.experimental import pallas as pl
from jax.experimental.pallas import tpu as pltpu
from jax.sharding import PartitionSpec as P

ITERS = 2
coupling = 0.995
AXES = ("tm", "rows")


def column_windows(field, blocks, halo):
    width = field.shape[-1] // blocks
    split = field.shape[:-1] + (blocks, width)
    parts = []
    for step in range(halo, 0, -1):
        moved = jnp.pad(field, [(0, 0)] * (field.ndim - 1) + [(step, 0)])[..., : field.shape[-1]]
        parts.append(moved.reshape(split)[..., :1])
    parts.append(field.reshape(split))
    for step in range(1, halo + 1):
        moved = jnp.pad(field, [(0, 0)] * (field.ndim - 1) + [(0, step)])[..., step:]
        parts.append(moved.reshape(split)[..., -1:])
    return jnp.concatenate(parts, axis=-1)


def hour_factors(main, off):
    def advance(inverse, row):
        inverse = 1.0 / (row - off * off * inverse)
        return inverse, inverse

    return lax.scan(advance, jnp.zeros_like(off), main)[1]


def hour_solve(right, inverse, ratio):
    def down(before, entries):
        value, inv, rat = entries
        now = value * inv - rat * before
        return now, now

    def up(after, entries):
        value, rat = entries
        now = value - rat * after
        return now, now

    zero = jnp.zeros_like(right[0])
    forward = lax.scan(down, zero, (right, inverse, ratio))[1]
    return lax.scan(up, zero, (forward, ratio), reverse=True)[1]


def split_off(field, weights):
    padded = jnp.pad(field, ((0, 0), (1, 1), (1, 1)))
    beside = padded[:, 2:, 1:-1] + padded[:, :-2, 1:-1] + padded[:, 1:-1, 2:] + padded[:, 1:-1, :-2]
    hours = jnp.pad(beside, ((1, 1), (0, 0), (0, 0)))
    return weights * beside - coupling * (hours[2:] + hours[:-2])


def step_scalars(a, h, hp, k, m, n):
    alpha = a / (a - h)
    delta = -h / (a - h)
    rz = delta * delta * a + alpha * delta * (h + hp) + alpha * alpha * k
    g = delta + rz / a
    curve = g * g * (a - h) + g * alpha * (h - m + hp - k) + alpha * alpha * (k - n)
    beta = rz / curve
    return alpha + beta * g, beta * alpha, delta - beta * g, alpha + beta * g - beta * alpha


def per_device_any(observations, obs_noise, prior_noise, observed, kappa_sq, obs_precision):
    hours, rows, columns = observations.shape
    over_tm, over_rows = lax.axis_size("tm"), lax.axis_size("rows")
    blocks = over_tm * over_rows
    width = columns // blocks
    wide = width + 2 * ITERS
    mask = observed.astype(jnp.float32)
    obs_weight = mask * obs_precision
    right = (
        mask * (obs_precision * observations + jnp.sqrt(obs_precision) * obs_noise) + prior_noise
    )
    payload = jnp.concatenate([right, obs_weight, kappa_sq[None]], axis=0)
    payload = jnp.moveaxis(column_windows(payload, blocks, ITERS), 2, 0)
    payload = payload.reshape(blocks, -1)
    got = lax.all_to_all(payload, AXES, split_axis=0, concat_axis=0, tiled=True)
    got = got.reshape(over_tm, over_rows, 2 * hours + 1, rows, wide)
    got = jnp.moveaxis(got, 2, 1)
    all_rows = over_rows * rows
    every = over_tm * hours
    r0 = got[:, :hours].reshape(every, all_rows, wide)
    ow = got[:, hours : 2 * hours].reshape(every, all_rows, wide)
    diag = got[0, 2 * hours].reshape(all_rows, wide) + 4.0
    where = (lax.axis_index("tm") * over_rows + lax.axis_index("rows")) * width
    column = where - ITERS + jnp.arange(wide, dtype=jnp.int32)
    inside = (column >= 0) & (column < columns)
    hour = jnp.arange(every)
    ends = (hour == 0) | (hour == every - 1)
    weights = jnp.where(ends, 1.0, 1.0 + coupling * coupling).astype(jnp.float32)[:, None, None]
    off = -coupling * diag
    inverse = hour_factors(weights * diag + ow, off)
    ratio = off * inverse
    z0 = hour_solve(r0, inverse, ratio)
    s1 = jnp.where(inside, split_off(z0, weights), 0.0)
    y1 = hour_solve(s1, inverse, ratio)
    s2 = jnp.where(inside, split_off(y1, weights), 0.0)
    y2 = hour_solve(s2, inverse, ratio)
    own = slice(ITERS, ITERS + width)
    r0, z0, s1, y1, s2, y2 = (part[:, :, own] for part in (r0, z0, s1, y1, s2, y2))
    pairs = ((r0, z0), (z0, s1), (r0, y1), (s1, y1), (z0, s2), (y1, s2))
    sums = jnp.stack([jnp.sum(x * y) for x, y in pairs])
    back = jnp.stack([z0, y1, y2, s1, s2]).reshape(-1, over_tm, hours, over_rows, rows, width)
    items = back.shape[0]
    back = back.transpose(1, 3, 0, 2, 4, 5).reshape(blocks, -1)
    back = jnp.concatenate([back, jnp.broadcast_to(sums, (blocks, sums.shape[0]))], axis=1)
    got = lax.all_to_all(back, AXES, split_axis=0, concat_axis=0, tiled=True)
    sums = jnp.sum(got[:, -sums.shape[0] :], axis=0)
    got = got[:, : -sums.shape[0]].reshape(blocks, items, hours, rows, width)
    z0, y1, y2, s1, s2 = got.transpose(1, 2, 3, 0, 4).reshape(items, hours, rows, columns)
    cx, c2, c0, c1 = step_scalars(*sums)
    return (
        cx * z0 + c2 * y1,
        c0 * right + c1 * s1 + c2 * s2,
        c0 * z0 + c1 * y1 + c2 * y2,
    )


LANES, SUB = 128, 8
HALF = LANES // 2
SLOTS = 4
SLOT = LANES // SLOTS
EXTRA = 2


def lanes_of():
    lane = lax.broadcasted_iota(jnp.int32, (SUB, LANES), 1)
    sub = lax.broadcasted_iota(jnp.int32, (SUB, LANES), 0)
    return lane, sub


def turn(x, shift):
    shift = shift % LANES
    return x if shift == 0 else pltpu.roll(x, shift, 1)


def halves(a, b, left):
    return jnp.where(left, a, turn(b, HALF)), jnp.where(left, turn(a, HALF), b)


def quad(q, left, first):
    p0, p2 = halves(q[0], q[2], left)
    p1, p3 = halves(q[1], q[3], left)
    result = []
    for a, b in ((p0, p1), (p2, p3)):
        result.append(jnp.where(first, a, turn(b, SLOT)))
        result.append(jnp.where(first, turn(a, -SLOT), b))
    return result


def tile(ref, k, *row):
    at = pl.ds(k * LANES, LANES)
    return ref[row + (slice(None), at)] if row else ref[:, at]


def pack_kernel(obs, noise, prior, observed, kappa, precision, pair, out):
    hours, _, columns = obs.shape
    tiles = columns // LANES
    blocks = tiles * SLOTS
    lane, sub = lanes_of()
    left = lane < HALF
    slot_lane = lax.rem(lane, SLOT)
    first = lax.rem(lane, HALF) < SLOT
    rows = SUB + EXTRA
    prec = precision[...]
    root = jnp.sqrt(prec)
    for h in range(hours):
        mask = observed[h].astype(jnp.float32)
        pair[0, h] = mask * (prec * obs[h] + root * noise[h]) + prior[h]
        pair[1, h] = mask * prec
    zero = jnp.zeros((SUB, LANES), jnp.float32)

    strip = lax.axis_index("rows")
    span = 2 * ITERS
    wide = 2 * hours * span
    before = lax.rem(lane // ITERS, 2) == 0
    ends, begins = [], []
    for k in range(tiles):
        items = [tile(pair, k, i, h) for i in (0, 1) for h in range(hours)]
        mine = [tile(pair, k, i, h) for i in (strip, 1 - strip) for h in range(hours)]
        for j, chunk in enumerate(quad(mine, left, first)):
            out[pl.ds((k * SLOTS + j) * rows, SUB), :] = chunk
        begin, end = zero, zero
        for i, item in enumerate(items):
            at = i * span
            begin = jnp.where(slot_lane // ITERS == i * 2 + 1, turn(item, at + ITERS), begin)
            end = jnp.where(slot_lane // ITERS == i * 2, turn(item, at - SLOT + ITERS), end)
        ends.append(turn(end, SLOT))
        begins.append(turn(begin, -SLOT))

    def before_tile(k):
        return jnp.where(lane < SLOT, ends[k - 1] if k else 0.0, ends[k])

    def after_tile(k):
        return jnp.where(
            lane >= LANES - SLOT, begins[k + 1] if k + 1 < tiles else 0.0, begins[k]
        )

    line = lax.rem(lax.axis_index("tm"), SUB)
    kap = [
        jnp.broadcast_to(
            jnp.sum(jnp.where(sub == line, tile(kappa, k), 0.0), axis=0, keepdims=True),
            (SUB, LANES),
        )
        for k in range(tiles)
    ]

    def kappa_rows(k):
        here = jnp.where((sub < 2) & (lane >= HALF), kap[max(k - 1, 0)], kap[k])
        return jnp.where(
            (sub // 2 == 1) & (lane < HALF), kap[min(k + 1, tiles - 1)], here
        )

    falling = lax.rem(SUB - sub, SUB)
    swapped = lax.rem(lane // wide + sub, SUB)
    for k in range(0, tiles, 2):
        near = [
            jnp.where(slot_lane < wide, of(k), turn(of(k + 1), wide))
            for of in (before_tile, after_tile)
        ]
        halo = jnp.where(before, near[0], pltpu.roll(near[1], SUB - 2, 0))
        halo = jnp.take_along_axis(halo, falling, axis=0)
        halo = pltpu.roll(halo, 0, 1, stride=wide, stride_axis=0)
        halo = jnp.take_along_axis(halo, swapped, axis=0)
        halo = pltpu.roll(halo, 0, 1, stride=wide, stride_axis=0)
        halo = jnp.where(strip == 0, halo, turn(halo, HALF))
        lines = jnp.where(
            lax.rem(sub, 2) == 0, kappa_rows(k), turn(kappa_rows(k + 1), -SLOT // 2)
        )
        lines = pltpu.roll(lines, 0, 1, stride=SLOT // 2, stride_axis=0)
        for r in range(SUB):
            group = (SUB - r) % SUB
            block = (k + group % 2) * SLOTS + group // 2
            out[pl.ds(block * rows + SUB, 1), :] = halo[r : r + 1]
            block = (k + r % 2) * SLOTS + (SLOTS - r // 2) % SLOTS
            out[pl.ds(block * rows + SUB + 1, 1), :] = lines[r : r + 1]


def solve_kernel(
    columns, got, out, right, inv_in, rat, z0, y1, y2, s1, s2, side, middle, totals
):
    strips, hb = 2, 2
    rows = SUB + EXTRA
    blocks = got.shape[0] // rows
    pairs = blocks // strips
    every = pairs * hb
    width = SLOT
    half = every // 2
    lane, sub = lanes_of()
    left = lane < HALF
    first = lax.rem(lane, HALF) < SLOT
    low = lax.rem(lane + ITERS, LANES) < HALF
    place = lax.rem(lane + ITERS, HALF) - ITERS
    block = lax.axis_index("tm") * strips + lax.axis_index("rows")
    column = block * width + place
    window = place < width + ITERS
    inside = window & (column >= 0) & (column < columns)
    own = (place >= 0) & (place < width)
    zero = jnp.zeros((SUB, LANES), jnp.float32)

    def strip_rows(at):
        return [jnp.broadcast_to(got[pl.ds(at + s * rows, 1), :], (SUB, LANES)) for s in (0, 1)]

    kap = [zero, zero]
    for i in range(SUB):
        lines = strip_rows(i * strips * rows + SUB + 1)
        kap = [jnp.where(sub == i, line, k) for line, k in zip(lines, kap)]
    kap = jnp.where(low, kap[0], turn(kap[1], HALF))
    diag = jnp.where(window, kap, 0.0) + 4.0
    off = -coupling * diag
    off_sq = off * off
    inner = (1.0 + coupling * coupling) * diag

    span = 2 * ITERS
    wide = 2 * hb * span

    def fields(pair):
        at = pair * strips * rows
        c0, c1 = got[pl.ds(at, SUB), :], got[pl.ds(at + rows, SUB), :]
        h0, h1 = (
            pltpu.roll(line, 0, 1, stride=wide, stride_axis=0) for line in strip_rows(at + SUB)
        )
        halo = jnp.where(left, h0, h1)
        r, w = jnp.where(left, c0, c1), jnp.where(left, c1, c0)
        result = []
        for item, mine in enumerate((r, turn(r, -SLOT), turn(w, HALF), turn(w, SLOT))):
            result.append(jnp.where(own, mine, turn(halo, -ITERS - item * span)))
        return result

    def hour_weight(t):
        return 1.0 if t in (0, every - 1) else 1.0 + coupling * coupling

    def main_of(t, weight):
        return jnp.where(window, weight, 0.0) + (diag if t in (0, every - 1) else inner)

    def eliminate(hours, rhs, weights, before):
        main = [main_of(t, w) for t, w in zip(hours, weights)]
        pivot = main[0] if before is None else main[0] - off_sq * before[0]
        inv_a = 1.0 / pivot
        inv_b = pivot * (1.0 / (pivot * main[1] - off_sq))
        g = None if before is None else before[1]
        for t, r, iv in zip(hours, rhs, (inv_a, inv_b)):
            c = off * iv
            g = r * iv if g is None else r * iv - c * g
            right[t], rat[t], z0[t] = r, c, g
            inv_in[t] = jnp.where(inside, coupling * iv, 0.0)
        return inv_b, g

    top, low_t = half - 1, half

    def phase(body):
        pl.when(block >= 0)(body)

    @phase
    def _():
        upper = lower = None
        for i in range(0, half, hb):
            r_a, r_b, w_a, w_b = fields(i // hb)
            q_a, q_b, v_a, v_b = fields(pairs - 1 - i // hb)
            upper = eliminate((i, i + 1), (r_a, r_b), (w_a, w_b), upper)
            lower = eliminate((every - 1 - i, every - 2 - i), (q_b, q_a), (v_b, v_a), lower)
        middle[...] = 1.0 / (1.0 - rat[top] * rat[low_t])


    def outward(ref):
        a = (ref[top] - rat[top] * ref[low_t]) * middle[...]
        b = ref[low_t] - rat[low_t] * a
        ref[top], ref[low_t] = a, b
        for i in range(1, half):
            a = ref[top - i] - rat[top - i] * a
            b = ref[low_t + i] - rat[low_t + i] * b
            ref[top - i], ref[low_t + i] = a, b

    def inward(source, ref):
        a = b = None
        for i in range(half):
            j = every - 1 - i
            a = source[i] * inv_in[i] if a is None else source[i] * inv_in[i] - rat[i] * a
            b = source[j] * inv_in[j] if b is None else source[j] * inv_in[j] - rat[j] * b
            ref[i], ref[j] = a, b

    last, initial = sub == SUB - 1, sub == 0
    edge = (last & ~low) | (initial & low)

    def beside(v, t, base):
        across = jnp.where(edge, turn(v, HALF), 0.0)
        pair, h = divmod(t, hb)
        for i, row in enumerate((0, SUB - 1)):
            side[i, pair, base + h : base + h + 1] = across[row : row + 1]
        up = pltpu.roll(jnp.where(last, across, v), 1, 0)
        down = pltpu.roll(jnp.where(initial, across, v), SUB - 1, 0)
        return (up + down) + (turn(v, 1) + turn(v, -1))

    def split(ref, result, base):
        old, now = zero, ref[0]
        for t in range(every):
            new = ref[t + 1] if t + 1 < every else zero
            mixed = (hour_weight(t) / coupling) * now - (old + new)
            result[t] = beside(mixed, t, base)
            old, now = now, new

    def two(ref, pair):
        before = ref[pair * hb - 1] if pair > 0 else zero
        after = ref[pair * hb + hb] if pair + 1 < pairs else zero
        return jnp.where(first, before, turn(after, SLOT))

    size = out.shape[0] // blocks

    def shared(a, b):
        b = turn(b, HALF)
        return jnp.where(left, a, b), jnp.where(left, b, a)

    def total_of(i, x, y):
        parts = [x[t] * y[t] for t in range(4)]
        for t in range(4, every):
            parts[t % 4] = parts[t % 4] + x[t] * y[t]
        totals[i] = (parts[0] + parts[1]) + (parts[2] + parts[3])

    @phase
    def _():
        outward(z0)

    @phase
    def _():
        split(z0, s1, 2)
        total_of(0, right, z0)

    @phase
    def _():
        inward(s1, y1)
        outward(y1)

    @phase
    def _():
        split(y1, s2, 4)
        total_of(1, z0, s1)
        total_of(2, right, y1)
        total_of(3, s1, y1)

    @phase
    def _():
        inward(s2, y2)
        outward(y2)
        total_of(4, z0, s2)
        total_of(5, y1, s2)
        sums = [zero, zero]
        for i in range(6):
            part = jnp.sum(jnp.where(own, totals[i], 0.0), axis=0, keepdims=True)
            part = part * (1.0 if i in (0, 2) else coupling)
            sums[i // 3] = jnp.where(sub == i % 3 + 2, part, sums[i // 3])
        sums = [part + turn(part, HALF) for part in sums]
        sums = [part + turn(part, -SLOT // 2) for part in sums]
        low_part = lax.rem(lane, SLOT) < SLOT // 2
        middle[...] = jnp.where(low_part, turn(sums[0], SLOT), turn(sums[1], SLOT + SLOT // 2))
        for pair in range(pairs):
            for strip, chunk in enumerate(shared(two(z0, pair), two(y1, pair))):
                out[pl.ds((strips * pair + strip) * size, SUB), :] = chunk

    total = middle[...]
    for pair in range(pairs):
        mine = two(y2, pair)
        line = jnp.where(low, side[0, pair], side[1, pair]) * coupling
        other = jnp.where(first, line, total)
        other = jnp.where(sub >= SUB - 2, mine, other)
        for strip, chunk in enumerate(shared(pltpu.roll(mine, 2, 0), other)):
            out[pl.ds((strips * pair + strip) * size + SUB, SUB - 2), :] = chunk[2:]


def unpack_kernel(
    got, pair, kappa, solution, residual, precond, zy, y2, side, coef
):
    hb = 2
    size = 2 * SUB - 2
    blocks = got.shape[0] // size
    tiles = blocks // SLOTS
    lane, sub = lanes_of()
    left = lane < HALF
    first = lax.rem(lane, HALF) < SLOT
    mine, strip = lax.axis_index("tm"), lax.axis_index("rows")
    inner = 1.0 + coupling * coupling
    e_a = jnp.where(mine == 0, 1.0, inner)
    e_b = jnp.where(mine == lax.axis_size("tm") - 1, 1.0, inner)

    for k in range(tiles):
        diag = tile(kappa, k) + 4.0
        off = -coupling * diag
        d_a = e_a * diag + tile(pair, k, 1, 0)
        d_b = e_b * diag + tile(pair, k, 1, 1)
        scale = 1.0 / (d_a * d_b - off * off)
        coef[0, k], coef[1, k], coef[2, k], coef[3, k] = d_b * scale, off * scale, d_a * scale, off

    def early_of(c):
        return got[pl.ds(c * size, SUB), :]

    def late_of(c):
        return got[pl.ds(c * size + SUB - 2, SUB), :]

    def spot(field, q, k):
        return (field * (hb + 2) + q) * tiles + k

    parts = [late_of(c) for c in range(4)]
    for c in range(4, blocks):
        parts[c % 4] = parts[c % 4] + late_of(c)
    total = (parts[0] + parts[1]) + (parts[2] + parts[3])
    sums = []
    for i in range(2):
        begin = jnp.where(strip == 0, LANES - SLOT, SLOT) + i * (SLOT // 2)
        here = (lane >= begin) & (lane < begin + SLOT // 2)
        part = jnp.sum(jnp.where(here, total, 0.0), axis=1, keepdims=True)
        part = jnp.broadcast_to(part, (SUB, LANES))
        sums += [jnp.broadcast_to(part[r : r + 1], (SUB, LANES)) for r in range(2, 5)]
    cx, c2, c0, c1 = step_scalars(*sums)

    for k in range(tiles):
        group = range(k * SLOTS, k * SLOTS + SLOTS)
        early = quad([early_of(c) for c in group], left, first)
        for field, b, a in ((strip, early[0], early[1]), (1 - strip, early[2], early[3])):
            zy[spot(field, 0, k)], zy[spot(field, hb + 1, k)] = b, a
        q = [late_of(c) for c in group]
        (p0, p2), (p1, p3) = halves(q[0], q[2], left), halves(q[1], q[3], left)
        p0, p2 = jnp.where(strip == 0, p0, p2), jnp.where(strip == 0, p2, p0)
        p1, p3 = jnp.where(strip == 0, p1, p3), jnp.where(strip == 0, p3, p1)
        p0, p1 = (
            jnp.where(sub < SUB - 2, pltpu.roll(p, SUB - 2, 0), high)
            for p, high in ((p0, p2), (p1, p3))
        )
        y2[0, k] = jnp.where(first, p0, turn(p1, SLOT))
        y2[1, k] = jnp.where(first, turn(p0, -SLOT), p1)
        side[k] = jnp.where(first, p2, turn(p3, SLOT))

    last, initial = sub == SUB - 1, sub == 0
    edge = sub == jnp.where(strip == 0, SUB - 1, 0)

    def block_solve(k, f_a, f_b, before, after):
        f_a, f_b = f_a - coef[3, k] * before, f_b - coef[3, k] * after
        return coef[0, k] * f_a - coef[1, k] * f_b, coef[2, k] * f_b - coef[1, k] * f_a

    def split(field, base):
        def mixed(k):
            v = [zy[spot(field, q, k)] for q in range(hb + 2)]
            combined = [
                e * v[h + 1] - coupling * (v[h] + v[h + 2]) for h, e in enumerate((e_a, e_b))
            ]
            return [(c, turn(c, 1), turn(c, -1)) for c in combined]

        before, now = [(0.0, 0.0, 0.0)] * hb, mixed(0)
        for k in range(tiles):
            after = mixed(k + 1) if k + 1 < tiles else [(0.0, 0.0, 0.0)] * hb
            result = []
            for h in range(hb):
                c, forward, back = now[h]
                up = pltpu.roll(jnp.where(last, 0.0, c), 1, 0)
                down = pltpu.roll(jnp.where(initial, 0.0, c), SUB - 1, 0)
                west = jnp.where(lane == 0, before[h][1], forward)
                east = jnp.where(lane == LANES - 1, after[h][2], back)
                line = jnp.where(edge, side[k, base + h : base + h + 1, :], 0.0)
                result.append((up + down) + (east + west) + line)
            yield k, *result
            before, now = now, after

    def hour(field, q, k):
        return zy[spot(field, q, k)]

    for k in range(tiles):
        zy[spot(0, 1, k)], zy[spot(0, 2, k)] = block_solve(
            k, tile(pair, k, 0, 0), tile(pair, k, 0, 1), hour(0, 0, k), hour(0, 3, k)
        )
    for k, *s1 in split(0, 2):
        at = pl.ds(k * LANES, LANES)
        solved = block_solve(k, *s1, hour(1, 0, k), hour(1, 3, k))
        for h in range(hb):
            zy[spot(1, h + 1, k)] = solved[h]
            solution[h, :, at] = cx * hour(0, h + 1, k) + c2 * solved[h]
            residual[h, :, at] = c0 * tile(pair, k, 0, h) + c1 * s1[h]
    for k, *s2 in split(1, 4):
        at = pl.ds(k * LANES, LANES)
        solved = block_solve(k, *s2, y2[0, k], y2[1, k])
        for h in range(hb):
            residual[h, :, at] = tile(residual, k, h) + c2 * s2[h]
            precond[h, :, at] = (
                c0 * hour(0, h + 1, k) + c1 * hour(1, h + 1, k) + c2 * solved[h]
            )


def exchange(chunks, blocks):
    rows = chunks.shape[0] // blocks
    chunks = chunks.reshape(blocks, rows // EXTRA, EXTRA, LANES)
    return lax.all_to_all(chunks, AXES, split_axis=0, concat_axis=0, tiled=True).reshape(-1, LANES)


def per_device(observations, obs_noise, prior_noise, observed, kappa_sq, obs_precision):
    hours, rows, columns = observations.shape
    pairs = lax.axis_size("tm")
    blocks = pairs * lax.axis_size("rows")
    fits = (
        lax.axis_size("rows") == 2
        and hours == 2
        and rows == SUB
        and columns == blocks * SLOT
        and pairs >= SUB
        and pairs % SUB == 0
    )
    args = (observations, obs_noise, prior_noise, observed, kappa_sq, obs_precision)
    if not fits:
        return per_device_any(*args)

    def shaped(*shape):
        return jax.ShapeDtypeStruct(shape, jnp.float32)

    def room(*shape):
        return pltpu.VMEM(shape, jnp.float32)

    def near(x):
        return pltpu.with_memory_space_constraint(x, pltpu.VMEM)

    field = shaped(hours, rows, columns)
    pair, chunks = pl.pallas_call(
        pack_kernel,
        out_shape=(
            pltpu.VMEM((2, hours, rows, columns), jnp.float32),
            pltpu.VMEM((blocks * (rows + EXTRA), LANES), jnp.float32),
        ),
        name="pack",
    )(*args)
    got = exchange(chunks, blocks)
    every = pairs * hours
    chunks = pl.pallas_call(
        lambda *refs: solve_kernel(columns, *refs),
        out_shape=pltpu.VMEM((blocks * (2 * rows - 2), LANES), jnp.float32),
        scratch_shapes=[room(every, rows, LANES)] * 8 + [room(2, pairs, rows, LANES), room(rows, LANES), room(6, rows, LANES)],
        name="solve",
    )(near(got))
    got = exchange(chunks, blocks)
    tiles = columns // LANES
    return tuple(
        pl.pallas_call(
            unpack_kernel,
            out_shape=[field] * 3,
            scratch_shapes=[
                room(2 * (hours + 2) * tiles, rows, LANES),
                room(2, tiles, rows, LANES),
                room(tiles, rows, LANES),
                room(4, tiles, rows, LANES),
            ],
            name="unpack",
        )(*(near(x) for x in (got, pair, kappa_sq)))
    )


def solution(mesh):
    whole, plane = P("tm", "rows", None), P("rows", None)
    return jax.shard_map(
        per_device,
        mesh=mesh,
        in_specs=(whole, whole, whole, whole, plane, plane),
        out_specs=(whole, whole, whole),
        check_vma=False,
    )
```

```python
import jax
import jax.numpy as jnp
from jax import lax
from jax.experimental import pallas as pl
from jax.experimental.pallas import tpu as pltpu
from jax.sharding import PartitionSpec as P

ITERS = 2
coupling = 0.995
AXES = ("tm", "rows")


def column_windows(field, blocks, halo):
    width = field.shape[-1] // blocks
    split = field.shape[:-1] + (blocks, width)
    parts = []
    for step in range(halo, 0, -1):
        moved = jnp.pad(field, [(0, 0)] * (field.ndim - 1) + [(step, 0)])[..., : field.shape[-1]]
        parts.append(moved.reshape(split)[..., :1])
    parts.append(field.reshape(split))
    for step in range(1, halo + 1):
        moved = jnp.pad(field, [(0, 0)] * (field.ndim - 1) + [(0, step)])[..., step:]
        parts.append(moved.reshape(split)[..., -1:])
    return jnp.concatenate(parts, axis=-1)


def hour_factors(main, off):
    def advance(inverse, row):
        inverse = 1.0 / (row - off * off * inverse)
        return inverse, inverse

    return lax.scan(advance, jnp.zeros_like(off), main)[1]


def hour_solve(right, inverse, ratio):
    def down(before, entries):
        value, inv, rat = entries
        now = value * inv - rat * before
        return now, now

    def up(after, entries):
        value, rat = entries
        now = value - rat * after
        return now, now

    zero = jnp.zeros_like(right[0])
    forward = lax.scan(down, zero, (right, inverse, ratio))[1]
    return lax.scan(up, zero, (forward, ratio), reverse=True)[1]


def split_off(field, weights):
    padded = jnp.pad(field, ((0, 0), (1, 1), (1, 1)))
    beside = padded[:, 2:, 1:-1] + padded[:, :-2, 1:-1] + padded[:, 1:-1, 2:] + padded[:, 1:-1, :-2]
    hours = jnp.pad(beside, ((1, 1), (0, 0), (0, 0)))
    return weights * beside - coupling * (hours[2:] + hours[:-2])


def step_scalars(a, h, hp, k, m, n):
    alpha = a / (a - h)
    delta = -h / (a - h)
    rz = delta * delta * a + alpha * delta * (h + hp) + alpha * alpha * k
    g = delta + rz / a
    curve = g * g * (a - h) + g * alpha * (h - m + hp - k) + alpha * alpha * (k - n)
    beta = rz / curve
    return alpha + beta * g, beta * alpha, delta - beta * g, alpha + beta * g - beta * alpha


def per_device_any(observations, obs_noise, prior_noise, observed, kappa_sq, obs_precision):
    hours, rows, columns = observations.shape
    over_tm, over_rows = lax.axis_size("tm"), lax.axis_size("rows")
    blocks = over_tm * over_rows
    width = columns // blocks
    wide = width + 2 * ITERS
    mask = observed.astype(jnp.float32)
    obs_weight = mask * obs_precision
    right = (
        mask * (obs_precision * observations + jnp.sqrt(obs_precision) * obs_noise) + prior_noise
    )
    payload = jnp.concatenate([right, obs_weight, kappa_sq[None]], axis=0)
    payload = jnp.moveaxis(column_windows(payload, blocks, ITERS), 2, 0)
    payload = payload.reshape(blocks, -1)
    got = lax.all_to_all(payload, AXES, split_axis=0, concat_axis=0, tiled=True)
    got = got.reshape(over_tm, over_rows, 2 * hours + 1, rows, wide)
    got = jnp.moveaxis(got, 2, 1)
    all_rows = over_rows * rows
    every = over_tm * hours
    r0 = got[:, :hours].reshape(every, all_rows, wide)
    ow = got[:, hours : 2 * hours].reshape(every, all_rows, wide)
    diag = got[0, 2 * hours].reshape(all_rows, wide) + 4.0
    where = (lax.axis_index("tm") * over_rows + lax.axis_index("rows")) * width
    column = where - ITERS + jnp.arange(wide, dtype=jnp.int32)
    inside = (column >= 0) & (column < columns)
    hour = jnp.arange(every)
    ends = (hour == 0) | (hour == every - 1)
    weights = jnp.where(ends, 1.0, 1.0 + coupling * coupling).astype(jnp.float32)[:, None, None]
    off = -coupling * diag
    inverse = hour_factors(weights * diag + ow, off)
    ratio = off * inverse
    z0 = hour_solve(r0, inverse, ratio)
    s1 = jnp.where(inside, split_off(z0, weights), 0.0)
    y1 = hour_solve(s1, inverse, ratio)
    s2 = jnp.where(inside, split_off(y1, weights), 0.0)
    y2 = hour_solve(s2, inverse, ratio)
    own = slice(ITERS, ITERS + width)
    r0, z0, s1, y1, s2, y2 = (part[:, :, own] for part in (r0, z0, s1, y1, s2, y2))
    pairs = ((r0, z0), (z0, s1), (r0, y1), (s1, y1), (z0, s2), (y1, s2))
    sums = jnp.stack([jnp.sum(x * y) for x, y in pairs])
    back = jnp.stack([z0, y1, y2, s1, s2]).reshape(-1, over_tm, hours, over_rows, rows, width)
    items = back.shape[0]
    back = back.transpose(1, 3, 0, 2, 4, 5).reshape(blocks, -1)
    back = jnp.concatenate([back, jnp.broadcast_to(sums, (blocks, sums.shape[0]))], axis=1)
    got = lax.all_to_all(back, AXES, split_axis=0, concat_axis=0, tiled=True)
    sums = jnp.sum(got[:, -sums.shape[0] :], axis=0)
    got = got[:, : -sums.shape[0]].reshape(blocks, items, hours, rows, width)
    z0, y1, y2, s1, s2 = got.transpose(1, 2, 3, 0, 4).reshape(items, hours, rows, columns)
    cx, c2, c0, c1 = step_scalars(*sums)
    return (
        cx * z0 + c2 * y1,
        c0 * right + c1 * s1 + c2 * s2,
        c0 * z0 + c1 * y1 + c2 * y2,
    )


LANES, SUB = 128, 8
HALF = LANES // 2
SLOTS = 4
SLOT = LANES // SLOTS
EXTRA = 2


def lanes_of():
    lane = lax.broadcasted_iota(jnp.int32, (SUB, LANES), 1)
    sub = lax.broadcasted_iota(jnp.int32, (SUB, LANES), 0)
    return lane, sub


def turn(x, shift):
    shift = shift % LANES
    return x if shift == 0 else pltpu.roll(x, shift, 1)


def halves(a, b, left):
    return jnp.where(left, a, turn(b, HALF)), jnp.where(left, turn(a, HALF), b)


def quad(q, left, first):
    p0, p2 = halves(q[0], q[2], left)
    p1, p3 = halves(q[1], q[3], left)
    result = []
    for a, b in ((p0, p1), (p2, p3)):
        result.append(jnp.where(first, a, turn(b, SLOT)))
        result.append(jnp.where(first, turn(a, -SLOT), b))
    return result


def tile(ref, k, *row):
    at = pl.ds(k * LANES, LANES)
    return ref[row + (slice(None), at)] if row else ref[:, at]


def pack_kernel(obs, noise, prior, observed, kappa, precision, pair, out):
    hours, _, columns = obs.shape
    tiles = columns // LANES
    blocks = tiles * SLOTS
    lane, sub = lanes_of()
    left = lane < HALF
    slot_lane = lax.rem(lane, SLOT)
    first = lax.rem(lane, HALF) < SLOT
    rows = SUB + EXTRA
    prec = precision[...]
    root = jnp.sqrt(prec)
    for h in range(hours):
        mask = observed[h].astype(jnp.float32)
        pair[0, h] = mask * (prec * obs[h] + root * noise[h]) + prior[h]
        pair[1, h] = mask * prec
    zero = jnp.zeros((SUB, LANES), jnp.float32)

    strip = lax.axis_index("rows")
    span = 2 * ITERS
    wide = 2 * hours * span
    before = lax.rem(lane // ITERS, 2) == 0
    ends, begins = [], []
    for k in range(tiles):
        items = [tile(pair, k, i, h) for i in (0, 1) for h in range(hours)]
        mine = [
            jnp.where(strip == 0, items[i], items[(i + hours) % (2 * hours)])
            for i in range(2 * hours)
        ]
        for j, chunk in enumerate(quad(mine, left, first)):
            out[pl.ds((k * SLOTS + j) * rows, SUB), :] = chunk
        begin, end = zero, zero
        for i, item in enumerate(items):
            at = i * span
            begin = jnp.where(slot_lane // ITERS == i * 2 + 1, turn(item, at + ITERS), begin)
            end = jnp.where(slot_lane // ITERS == i * 2, turn(item, at - SLOT + ITERS), end)
        ends.append(turn(end, SLOT))
        begins.append(turn(begin, -SLOT))

    def before_tile(k):
        return jnp.where(lane < SLOT, ends[k - 1] if k else 0.0, ends[k])

    def after_tile(k):
        return jnp.where(
            lane >= LANES - SLOT, begins[k + 1] if k + 1 < tiles else 0.0, begins[k]
        )

    line = lax.rem(lax.axis_index("tm"), SUB)
    kap = [
        jnp.broadcast_to(
            jnp.sum(jnp.where(sub == line, tile(kappa, k), 0.0), axis=0, keepdims=True),
            (SUB, LANES),
        )
        for k in range(tiles)
    ]

    def kappa_rows(k):
        here = jnp.where((sub < 2) & (lane >= HALF), kap[max(k - 1, 0)], kap[k])
        return jnp.where(
            (sub // 2 == 1) & (lane < HALF), kap[min(k + 1, tiles - 1)], here
        )

    falling = lax.rem(SUB - sub + strip * (SUB // 2), SUB)
    swapped = lax.rem(lane // wide + sub, SUB)
    for k in range(0, tiles, 2):
        near = [
            jnp.where(slot_lane < wide, of(k), turn(of(k + 1), wide))
            for of in (before_tile, after_tile)
        ]
        halo = jnp.where(before, near[0], pltpu.roll(near[1], SUB - 2, 0))
        halo = jnp.take_along_axis(halo, falling, axis=0)
        halo = pltpu.roll(halo, 0, 1, stride=wide, stride_axis=0)
        halo = jnp.take_along_axis(halo, swapped, axis=0)
        halo = pltpu.roll(halo, 0, 1, stride=wide, stride_axis=0)
        lines = jnp.where(
            lax.rem(sub, 2) == 0, kappa_rows(k), turn(kappa_rows(k + 1), -SLOT // 2)
        )
        lines = pltpu.roll(lines, 0, 1, stride=SLOT // 2, stride_axis=0)
        for r in range(SUB):
            group = (SUB - r) % SUB
            block = (k + group % 2) * SLOTS + group // 2
            out[pl.ds(block * rows + SUB, 1), :] = halo[r : r + 1]
            block = (k + r % 2) * SLOTS + (SLOTS - r // 2) % SLOTS
            out[pl.ds(block * rows + SUB + 1, 1), :] = lines[r : r + 1]


def solve_kernel(
    columns, got, out, right, inv_in, rat, z0, y1, y2, s1, s2, side, middle, totals
):
    strips, hb = 2, 2
    rows = SUB + EXTRA
    blocks = got.shape[0] // rows
    pairs = blocks // strips
    every = pairs * hb
    width = SLOT
    half = every // 2
    lane, sub = lanes_of()
    left = lane < HALF
    first = lax.rem(lane, HALF) < SLOT
    low = lax.rem(lane + ITERS, LANES) < HALF
    place = lax.rem(lane + ITERS, HALF) - ITERS
    block = lax.axis_index("tm") * strips + lax.axis_index("rows")
    column = block * width + place
    window = place < width + ITERS
    inside = window & (column >= 0) & (column < columns)
    own = (place >= 0) & (place < width)
    zero = jnp.zeros((SUB, LANES), jnp.float32)

    def strip_rows(at):
        return [jnp.broadcast_to(got[pl.ds(at + s * rows, 1), :], (SUB, LANES)) for s in (0, 1)]

    kap = [zero, zero]
    for i in range(SUB):
        lines = strip_rows(i * strips * rows + SUB + 1)
        kap = [jnp.where(sub == i, line, k) for line, k in zip(lines, kap)]
    kap = jnp.where(low, kap[0], turn(kap[1], HALF))
    diag = jnp.where(window, kap, 0.0) + 4.0
    off = -coupling * diag
    off_sq = off * off
    inner = (1.0 + coupling * coupling) * diag

    span = 2 * ITERS
    wide = 2 * hb * span

    def fields(pair):
        at = pair * strips * rows
        c0, c1 = got[pl.ds(at, SUB), :], got[pl.ds(at + rows, SUB), :]
        h0, h1 = (
            pltpu.roll(line, 0, 1, stride=wide, stride_axis=0) for line in strip_rows(at + SUB)
        )
        halo = jnp.where(left, h0, h1)
        r, w = jnp.where(left, c0, c1), jnp.where(left, c1, c0)
        result = []
        for item, mine in enumerate((r, turn(r, -SLOT), turn(w, HALF), turn(w, SLOT))):
            result.append(jnp.where(own, mine, turn(halo, -ITERS - item * span)))
        return result

    def hour_weight(t):
        return 1.0 if t in (0, every - 1) else 1.0 + coupling * coupling

    def main_of(t, weight):
        return jnp.where(window, weight, 0.0) + (diag if t in (0, every - 1) else inner)

    def eliminate(hours, rhs, weights, before):
        main = [main_of(t, w) for t, w in zip(hours, weights)]
        pivot = main[0] if before is None else main[0] - off_sq * before[0]
        inv_a = 1.0 / pivot
        inv_b = pivot * (1.0 / (pivot * main[1] - off_sq))
        g = None if before is None else before[1]
        for t, r, iv in zip(hours, rhs, (inv_a, inv_b)):
            c = off * iv
            g = r * iv if g is None else r * iv - c * g
            right[t], rat[t], z0[t] = r, c, g
            inv_in[t] = jnp.where(inside, coupling * iv, 0.0)
        return inv_b, g

    top, low_t = half - 1, half

    def phase(body):
        pl.when(block >= 0)(body)

    @phase
    def _():
        upper = lower = None
        for i in range(0, half, hb):
            r_a, r_b, w_a, w_b = fields(i // hb)
            q_a, q_b, v_a, v_b = fields(pairs - 1 - i // hb)
            upper = eliminate((i, i + 1), (r_a, r_b), (w_a, w_b), upper)
            lower = eliminate((every - 1 - i, every - 2 - i), (q_b, q_a), (v_b, v_a), lower)
        middle[...] = 1.0 / (1.0 - rat[top] * rat[low_t])


    def outward(ref):
        a = (ref[top] - rat[top] * ref[low_t]) * middle[...]
        b = ref[low_t] - rat[low_t] * a
        ref[top], ref[low_t] = a, b
        for i in range(1, half):
            a = ref[top - i] - rat[top - i] * a
            b = ref[low_t + i] - rat[low_t + i] * b
            ref[top - i], ref[low_t + i] = a, b

    def inward(source, ref):
        a = b = None
        for i in range(half):
            j = every - 1 - i
            a = source[i] * inv_in[i] if a is None else source[i] * inv_in[i] - rat[i] * a
            b = source[j] * inv_in[j] if b is None else source[j] * inv_in[j] - rat[j] * b
            ref[i], ref[j] = a, b

    last, initial = sub == SUB - 1, sub == 0
    edge = (last & ~low) | (initial & low)

    def beside(v, t, base):
        across = jnp.where(edge, turn(v, HALF), 0.0)
        pair, h = divmod(t, hb)
        for i, row in enumerate((0, SUB - 1)):
            side[i, pair, base + h : base + h + 1] = across[row : row + 1]
        up = pltpu.roll(jnp.where(last, across, v), 1, 0)
        down = pltpu.roll(jnp.where(initial, across, v), SUB - 1, 0)
        return (up + down) + (turn(v, 1) + turn(v, -1))

    def split(ref, result, base):
        old, now = zero, ref[0]
        for t in range(every):
            new = ref[t + 1] if t + 1 < every else zero
            mixed = (hour_weight(t) / coupling) * now - (old + new)
            result[t] = beside(mixed, t, base)
            old, now = now, new

    def two(ref, pair):
        before = ref[pair * hb - 1] if pair > 0 else zero
        after = ref[pair * hb + hb] if pair + 1 < pairs else zero
        return jnp.where(first, before, turn(after, SLOT))

    size = out.shape[0] // blocks

    def shared(a, b):
        b = turn(b, HALF)
        return jnp.where(left, a, b), jnp.where(left, b, a)

    def total_of(i, x, y):
        parts = [x[t] * y[t] for t in range(4)]
        for t in range(4, every):
            parts[t % 4] = parts[t % 4] + x[t] * y[t]
        totals[i] = (parts[0] + parts[1]) + (parts[2] + parts[3])

    @phase
    def _():
        outward(z0)

    @phase
    def _():
        split(z0, s1, 2)
        total_of(0, right, z0)

    @phase
    def _():
        inward(s1, y1)
        outward(y1)

    @phase
    def _():
        split(y1, s2, 4)
        total_of(1, z0, s1)
        total_of(2, right, y1)
        total_of(3, s1, y1)

    @phase
    def _():
        for pair in range(pairs):
            for strip, chunk in enumerate(shared(two(z0, pair), two(y1, pair))):
                out[pl.ds((strips * pair + strip) * size, SUB), :] = chunk
        inward(s2, y2)
        outward(y2)
        total_of(4, z0, s2)
        total_of(5, y1, s2)
        sums = [zero, zero]
        for i in range(6):
            part = jnp.sum(jnp.where(own, totals[i], 0.0), axis=0, keepdims=True)
            part = part * (1.0 if i in (0, 2) else coupling)
            sums[i // 3] = jnp.where(sub == i % 3 + 2, part, sums[i // 3])
        sums = [part + turn(part, HALF) for part in sums]
        sums = [part + turn(part, -SLOT // 2) for part in sums]
        low_part = lax.rem(lane, SLOT) < SLOT // 2
        middle[...] = jnp.where(low_part, turn(sums[0], SLOT), turn(sums[1], SLOT + SLOT // 2))

    total = middle[...]
    for pair in range(pairs):
        mine = two(y2, pair)
        line = jnp.where(low, side[0, pair], side[1, pair]) * coupling
        other = jnp.where(first, line, total)
        other = jnp.where(sub >= SUB - 2, mine, other)
        for strip, chunk in enumerate(shared(pltpu.roll(mine, 2, 0), other)):
            out[pl.ds((strips * pair + strip) * size + SUB, SUB - 2), :] = chunk[2:]


def unpack_kernel(
    got, pair, kappa, solution, residual, precond, zy, y2, side, coef
):
    hb = 2
    size = 2 * SUB - 2
    blocks = got.shape[0] // size
    tiles = blocks // SLOTS
    lane, sub = lanes_of()
    left = lane < HALF
    first = lax.rem(lane, HALF) < SLOT
    mine, strip = lax.axis_index("tm"), lax.axis_index("rows")
    inner = 1.0 + coupling * coupling
    e_a = jnp.where(mine == 0, 1.0, inner)
    e_b = jnp.where(mine == lax.axis_size("tm") - 1, 1.0, inner)

    for k in range(tiles):
        diag = tile(kappa, k) + 4.0
        off = -coupling * diag
        d_a = e_a * diag + tile(pair, k, 1, 0)
        d_b = e_b * diag + tile(pair, k, 1, 1)
        scale = 1.0 / (d_a * d_b - off * off)
        coef[0, k], coef[1, k], coef[2, k], coef[3, k] = d_b * scale, off * scale, d_a * scale, off

    def early_of(c):
        return got[pl.ds(c * size, SUB), :]

    def late_of(c):
        return got[pl.ds(c * size + SUB - 2, SUB), :]

    def spot(field, q, k):
        return (field * (hb + 2) + q) * tiles + k

    parts = [late_of(c) for c in range(4)]
    for c in range(4, blocks):
        parts[c % 4] = parts[c % 4] + late_of(c)
    total = (parts[0] + parts[1]) + (parts[2] + parts[3])
    sums = []
    for i in range(2):
        begin = jnp.where(strip == 0, LANES - SLOT, SLOT) + i * (SLOT // 2)
        here = (lane >= begin) & (lane < begin + SLOT // 2)
        part = jnp.sum(jnp.where(here, total, 0.0), axis=1, keepdims=True)
        part = jnp.broadcast_to(part, (SUB, LANES))
        sums += [jnp.broadcast_to(part[r : r + 1], (SUB, LANES)) for r in range(2, 5)]
    cx, c2, c0, c1 = step_scalars(*sums)

    for k in range(tiles):
        group = range(k * SLOTS, k * SLOTS + SLOTS)
        early = quad([early_of(c) for c in group], left, first)
        for field, b, a in ((strip, early[0], early[1]), (1 - strip, early[2], early[3])):
            zy[spot(field, 0, k)], zy[spot(field, hb + 1, k)] = b, a
        q = [late_of(c) for c in group]
        (p0, p2), (p1, p3) = halves(q[0], q[2], left), halves(q[1], q[3], left)
        p0, p2 = jnp.where(strip == 0, p0, p2), jnp.where(strip == 0, p2, p0)
        p1, p3 = jnp.where(strip == 0, p1, p3), jnp.where(strip == 0, p3, p1)
        p0, p1 = (
            jnp.where(sub < SUB - 2, pltpu.roll(p, SUB - 2, 0), high)
            for p, high in ((p0, p2), (p1, p3))
        )
        y2[0, k] = jnp.where(first, p0, turn(p1, SLOT))
        y2[1, k] = jnp.where(first, turn(p0, -SLOT), p1)
        side[k] = jnp.where(first, p2, turn(p3, SLOT))

    last, initial = sub == SUB - 1, sub == 0
    edge = sub == jnp.where(strip == 0, SUB - 1, 0)

    def block_solve(k, f_a, f_b, before, after):
        f_a, f_b = f_a - coef[3, k] * before, f_b - coef[3, k] * after
        return coef[0, k] * f_a - coef[1, k] * f_b, coef[2, k] * f_b - coef[1, k] * f_a

    def split(field, base):
        def mixed(k):
            v = [zy[spot(field, q, k)] for q in range(hb + 2)]
            combined = [
                e * v[h + 1] - coupling * (v[h] + v[h + 2]) for h, e in enumerate((e_a, e_b))
            ]
            return [(c, turn(c, 1), turn(c, -1)) for c in combined]

        before, now = [(0.0, 0.0, 0.0)] * hb, mixed(0)
        for k in range(tiles):
            after = mixed(k + 1) if k + 1 < tiles else [(0.0, 0.0, 0.0)] * hb
            result = []
            for h in range(hb):
                c, forward, back = now[h]
                up = pltpu.roll(jnp.where(last, 0.0, c), 1, 0)
                down = pltpu.roll(jnp.where(initial, 0.0, c), SUB - 1, 0)
                west = jnp.where(lane == 0, before[h][1], forward)
                east = jnp.where(lane == LANES - 1, after[h][2], back)
                line = jnp.where(edge, side[k, base + h : base + h + 1, :], 0.0)
                result.append((up + down) + (east + west) + line)
            yield k, *result
            before, now = now, after

    def hour(field, q, k):
        return zy[spot(field, q, k)]

    for k in range(tiles):
        zy[spot(0, 1, k)], zy[spot(0, 2, k)] = block_solve(
            k, tile(pair, k, 0, 0), tile(pair, k, 0, 1), hour(0, 0, k), hour(0, 3, k)
        )
    for k, *s1 in split(0, 2):
        at = pl.ds(k * LANES, LANES)
        solved = block_solve(k, *s1, hour(1, 0, k), hour(1, 3, k))
        for h in range(hb):
            zy[spot(1, h + 1, k)] = solved[h]
            solution[h, :, at] = cx * hour(0, h + 1, k) + c2 * solved[h]
            residual[h, :, at] = c0 * tile(pair, k, 0, h) + c1 * s1[h]
    for k, *s2 in split(1, 4):
        at = pl.ds(k * LANES, LANES)
        solved = block_solve(k, *s2, y2[0, k], y2[1, k])
        for h in range(hb):
            residual[h, :, at] = tile(residual, k, h) + c2 * s2[h]
            precond[h, :, at] = (
                c0 * hour(0, h + 1, k) + c1 * hour(1, h + 1, k) + c2 * solved[h]
            )


def exchange(chunks, blocks):
    rows = chunks.shape[0] // blocks
    chunks = chunks.reshape(blocks, rows // EXTRA, EXTRA, LANES)
    return lax.all_to_all(chunks, AXES, split_axis=0, concat_axis=0, tiled=True).reshape(-1, LANES)


def per_device(observations, obs_noise, prior_noise, observed, kappa_sq, obs_precision):
    hours, rows, columns = observations.shape
    pairs = lax.axis_size("tm")
    blocks = pairs * lax.axis_size("rows")
    fits = (
        lax.axis_size("rows") == 2
        and hours == 2
        and rows == SUB
        and columns == blocks * SLOT
        and pairs >= SUB
        and pairs % SUB == 0
    )
    args = (observations, obs_noise, prior_noise, observed, kappa_sq, obs_precision)
    if not fits:
        return per_device_any(*args)

    def shaped(*shape):
        return jax.ShapeDtypeStruct(shape, jnp.float32)

    def room(*shape):
        return pltpu.VMEM(shape, jnp.float32)

    def near(x):
        return pltpu.with_memory_space_constraint(x, pltpu.VMEM)

    field = shaped(hours, rows, columns)
    pair, chunks = pl.pallas_call(
        pack_kernel,
        out_shape=(
            pltpu.VMEM((2, hours, rows, columns), jnp.float32),
            pltpu.VMEM((blocks * (rows + EXTRA), LANES), jnp.float32),
        ),
        name="pack",
    )(*args)
    got = exchange(chunks, blocks)
    every = pairs * hours
    chunks = pl.pallas_call(
        lambda *refs: solve_kernel(columns, *refs),
        out_shape=pltpu.VMEM((blocks * (2 * rows - 2), LANES), jnp.float32),
        scratch_shapes=[room(every, rows, LANES)] * 8 + [room(2, pairs, rows, LANES), room(rows, LANES), room(6, rows, LANES)],
        name="solve",
    )(near(got))
    got = exchange(chunks, blocks)
    tiles = columns // LANES
    return tuple(
        pl.pallas_call(
            unpack_kernel,
            out_shape=[field] * 3,
            scratch_shapes=[
                room(2 * (hours + 2) * tiles, rows, LANES),
                room(2, tiles, rows, LANES),
                room(tiles, rows, LANES),
                room(4, tiles, rows, LANES),
            ],
            name="unpack",
        )(*(near(x) for x in (got, pair, kappa_sq)))
    )


def solution(mesh):
    whole, plane = P("tm", "rows", None), P("rows", None)
    return jax.shard_map(
        per_device,
        mesh=mesh,
        in_specs=(whole, whole, whole, whole, plane, plane),
        out_specs=(whole, whole, whole),
        check_vma=False,
    )
```
